512 devices in a mesh: az: 8 (over z_lo), rz: 64 (over x, z_hi, y, core).
Axes of the slice: x: 4, y: 4, z: 16 (z_hi: 2, z_lo: 8; z = z_hi * 8 + z_lo), core: 2. Of those that a mesh axis runs over, the one named last changes fastest.
Arguments:
- positions: float32 [3, 2097152], P(None, ('az', 'rz')), may hold values from -32 to 72, as said below
- velocities: float32 [3, 2097152], P(None, ('az', 'rz')), may hold values from -6 to 6
- masses: bfloat16 [2097152], P(('az', 'rz')), may hold values from 0.5 to 2
- cells: int32 [2097152], P(('az', 'rz')), may hold values from 0 to 16383
- active: int32 [2097152], P(('az', 'rz')), may hold values 0 or 1
- send_lists: int32 [2, 131072], P(None, ('az', 'rz')), may hold values from 0 to 4095, as said below
- send_counts: int32 [2, 512], P(None, ('az', 'rz')), may hold values from 1 to 256, as said below
Outputs:
- potential: float32 [64, 64, 2048], P(None, 'rz', 'az')
- star_state: float32 [6, 2097152], P(None, ('az', 'rz'))
- arrivals: float32 [2, 7, 131072], P(None, None, ('az', 'rz'))
The draws below stay inside these ranges and needn't reach their ends.
Inputs may be any that keep to these rules, and one draw needn't show every extreme that they name: `positions`: row 0 is a radius between 8 and 72, row 1 an angle between 0 and 2 pi, row 2 a height between -32 and 32. `send_lists`: the two lists of a block name 512 different stars of that block, as indices within the block. `send_counts`: in each list row some block uses all 256 entries.
All inputs are finite; a program needn't handle non-finite values. No bound on the sum of `active` on one device may be relied on, other than what follows from the above.
Results may differ from the reference program's by a relative error of at most 0.0003.
Values sent between devices are 32-bit elements; how exact they have to be, the bound alone decides.
No kernel may reach another device: no remote copies, remote signals or barrier semaphores. Data moves between devices by JAX's collectives and lax.ppermute only.
A program may use at most 128 MiB of HBM per device.

```python
import math
import jax
import jax.numpy as jnp
from jax import lax

HEIGHTS = 64
AZIM = 2048
R_DEV = 1
S_DEV = 4096
AZ_DEV = 256
RADII = 64
CAP = 256
BLOCKS = 512
STARS = 2097152
N_AZ = 8
N_RZ = 64


def draw_positions(key, part):
    subkeys = jax.random.split(key, 3)
    radius = 8.0 + jax.random.uniform(subkeys[0], (STARS,), jnp.float32) * RADII
    azimuth = jax.random.uniform(subkeys[1], (STARS,), jnp.float32) * (2.0 * math.pi)
    height = (jax.random.uniform(subkeys[2], (STARS,), jnp.float32) - 0.5) * HEIGHTS
    return jnp.stack([radius, azimuth, height])


def draw_send_lists(key, part):
    blocks_all = STARS // S_DEV
    subkeys = jax.random.split(key, blocks_all)

    def choose(subkey):
        return jax.random.permutation(subkey, S_DEV)[:2 * CAP]
    chosen = jax.vmap(choose)(subkeys)
    return chosen.reshape(blocks_all, 2, CAP).transpose(1, 0, 2).reshape(2, blocks_all * CAP).astype(jnp.int32)


def draw_send_counts(key, part):
    blocks_all = STARS // S_DEV
    drawn = jax.random.randint(key, (2, blocks_all), 1, CAP + 1)
    fullest = jax.random.randint(jax.random.fold_in(key, 7), (2, 1), 0, blocks_all)
    places = jnp.arange(blocks_all, dtype=jnp.int32)[None, :]
    return jnp.where(places == fullest, CAP, drawn).astype(jnp.int32)


def set_ends(array, rng, least, high):
    longest = array.shape.index(max(array.shape))
    spots = []
    for shift in (0, 1):
        where = [jax.random.randint(jax.random.fold_in(rng, axis), (), 0, length) for axis, length in enumerate(array.shape)]
        where[longest] = (where[longest] + shift) % array.shape[longest]
        spots.append(tuple(where))
    return array.at[spots[0]].set(least).at[spots[1]].set(high)


def shard_levels(stream_key, extent, shards, smallest, largest):
    level, own = 1.0, jax.random.fold_in(stream_key, 6)
    for dim, shards_of in shards:
        heights = jnp.exp(jax.random.uniform(jax.random.fold_in(own, dim), (shards_of,), jnp.float32, smallest / len(shards), largest / len(shards)))
        level = level * jnp.repeat(heights, extent[dim] // shards_of).reshape([-1 if axis == dim else 1 for axis in range(len(extent))])
    return level


def bell_draw(rng, shape, spread, reach, pieces=(), held_as=jnp.bfloat16):
    values = spread * jax.random.normal(rng, shape, jnp.float32)
    if pieces:
        values = values * shard_levels(rng, shape, pieces, -0.22, 0.18)
    return jnp.clip(values, -reach, reach).astype(held_as)


def setup_inputs(seed: int = 0) -> dict:
    keys = jax.random.split(jax.random.key(seed), 8)
    return {
        "positions": draw_positions(jax.random.fold_in(keys[7], 71), 0),
        "velocities": bell_draw(keys[1], (3, STARS), 1.0, 6.0, ((1, 512),), jnp.float32),
        "masses": jnp.clip(jnp.exp(math.log(2.0) - 1.3862944 * jax.random.uniform(keys[2], (STARS,), jnp.float32) ** shard_levels(keys[2], (STARS,), ((0, 512),), -0.2, 0.2)), 0.5, 2.0).astype(jnp.bfloat16),
        "cells": set_ends(jax.random.randint(keys[3], (STARS,), 0, HEIGHTS * R_DEV * AZ_DEV), jax.random.fold_in(keys[3], 1), 0, (HEIGHTS * R_DEV * AZ_DEV) - 1).astype(jnp.int32),
        "active": set_ends((jax.random.randint(keys[4], (STARS,), 0, 2) < 1).astype(jnp.int32), jax.random.fold_in(keys[4], 1), 0, 1),
        "send_lists": draw_send_lists(jax.random.fold_in(keys[7], 71), 0),
        "send_counts": draw_send_counts(jax.random.fold_in(keys[7], 71), 0),
    }


two_pi = 2.0 * math.pi
inner_radius = 8.0
gravity = 1.0
time_step = 1.0

def cas_table(first, second, total):
    turns = first[:, None] * second[None, :] % total
    theta = turns.astype(jnp.float32) * (two_pi / total)
    return jnp.cos(theta) + jnp.sin(theta)

def slope_table(modes, angles, total):
    turns = modes[:, None] * angles[None, :] % total
    theta = turns.astype(jnp.float32) * (two_pi / total)
    signed = jnp.where(2 * modes < total, modes, modes - total)
    signed = jnp.where(2 * modes == total, 0, signed).astype(jnp.float32)
    return signed[:, None] * (jnp.cos(theta) - jnp.sin(theta))

def sine_table(count):
    levels = jnp.arange(count, dtype=jnp.int32) + 1
    turns = levels[:, None] * levels[None, :] % (2 * (count + 1))
    return math.sqrt(2.0 / (count + 1)) * jnp.sin(turns.astype(jnp.float32) * (math.pi / (count + 1)))

def vertical_eigen(count):
    levels = jnp.arange(count, dtype=jnp.int32).astype(jnp.float32) + 1.0
    return (2.0 * jnp.sin(levels * (math.pi / (2 * (count + 1))))) ** 2

def reference(positions, velocities, masses, cells, active, send_lists, send_counts):
    highest = lax.Precision.HIGHEST
    star_block = jnp.arange(STARS, dtype=jnp.int32) // S_DEV
    block_az = star_block // N_RZ
    block_rz = star_block % N_RZ
    plane = R_DEV * AZ_DEV
    height_of = cells // plane
    radius_of = cells % plane // AZ_DEV + block_rz * R_DEV
    angle_of = cells % AZ_DEV + block_az * AZ_DEV
    flat_cell = (height_of * RADII + radius_of) * AZIM + angle_of
    density = jax.ops.segment_sum(masses.astype(jnp.float32), flat_cell, num_segments=HEIGHTS * RADII * AZIM)
    sine = sine_table(HEIGHTS)
    layered = jnp.dot(sine, density.reshape(HEIGHTS, RADII * AZIM), precision=highest)
    indices = jnp.arange(AZIM, dtype=jnp.int32)
    hartley = cas_table(indices, indices, AZIM)
    spectrum = jnp.dot(layered.reshape(HEIGHTS * RADII, AZIM), hartley, precision=highest)
    source = (-gravity * spectrum).reshape(HEIGHTS, RADII, AZIM).transpose(1, 0, 2)
    radii = inner_radius + jnp.arange(RADII, dtype=jnp.int32).astype(jnp.float32) + 0.5
    eigen = vertical_eigen(HEIGHTS)
    modes = jnp.minimum(indices, AZIM - indices).astype(jnp.float32)

    def forward(state, bundle):
        upper_prev, value_prev = state
        radius, right_side = bundle
        lower = -(radius - 0.5) / radius
        upper = -(radius + 0.5) / radius
        diagonal = 2.0 + (modes * modes)[None, :] / (radius * radius) + eigen[:, None]
        denom = diagonal - lower * upper_prev
        upper_next = upper / denom
        value_next = (right_side - lower * value_prev) / denom
        return ((upper_next, value_next), (upper_next, value_next))
    empty = jnp.zeros((HEIGHTS, AZIM), jnp.float32)
    ignored, (factors, values) = lax.scan(forward, (empty, empty), (radii, source))

    def backward(later_value, bundle):
        factor, value = bundle
        current = value - factor * later_value
        return (current, current)
    ignored, solved = lax.scan(backward, empty, (factors, values), reverse=True)
    spectral = solved.transpose(1, 0, 2)
    potential_layers = jnp.dot(sine, spectral.reshape(HEIGHTS, RADII * AZIM), precision=highest).reshape(HEIGHTS * RADII, AZIM)
    potential = (jnp.dot(potential_layers, hartley, precision=highest) / AZIM).reshape(HEIGHTS, RADII, AZIM)
    angular = (jnp.dot(potential_layers, slope_table(indices, indices, AZIM), precision=highest) / AZIM).reshape(HEIGHTS, RADII, AZIM)
    padded = jnp.pad(potential, ((0, 0), (1, 1), (0, 0)))
    radial = (padded[:, 2:] - padded[:, :-2]) * 0.5
    padded = jnp.pad(potential, ((1, 1), (0, 0), (0, 0)))
    vertical = (padded[2:] - padded[:-2]) * 0.5
    radius_now = positions[0]
    accel = jnp.stack([-radial.reshape(-1)[flat_cell], -angular.reshape(-1)[flat_cell] / radius_now, -vertical.reshape(-1)[flat_cell]])
    live = active.astype(jnp.float32)
    new_velocities = velocities + time_step * live[None, :] * accel
    motion = jnp.stack([new_velocities[0], new_velocities[1] / radius_now, new_velocities[2]])
    new_positions = positions + time_step * live[None, :] * motion
    star_state = jnp.concatenate([new_positions, new_velocities], axis=0)
    moving = jnp.concatenate([star_state, masses.astype(jnp.float32)[None, :]], axis=0)
    grouped = moving.reshape(7, BLOCKS, S_DEV)
    lists = send_lists.reshape(2, BLOCKS, CAP)

    def pick(members, chosen):
        return members[:, chosen]
    picked = jax.vmap(pick, in_axes=(1, 1), out_axes=0)(grouped, lists)
    keep = jnp.arange(CAP, dtype=jnp.int32)[None, None, :] < send_counts.T[:, :, None]
    picked = picked * keep[:, None, :, :].astype(jnp.float32)
    picked = picked.reshape(N_AZ, N_RZ, 7, 2, CAP)
    from_lower = jnp.roll(picked[:, :, :, 1, :], 1, axis=0)
    from_upper = jnp.roll(picked[:, :, :, 0, :], -1, axis=0)
    arrivals = jnp.stack([from_lower, from_upper]).transpose(0, 3, 1, 2, 4).reshape(2, 7, BLOCKS * CAP)
    return (potential, star_state, arrivals)
```

```python
import functools
import math

import jax
import jax.numpy as jnp
import numpy as np
from jax import lax
from jax.experimental import pallas as pl
from jax.experimental.pallas import tpu as pltpu
from jax.sharding import Mesh
from jax.sharding import PartitionSpec as P

HEIGHTS = 64
RADII = 64
AZIM = 2048
SECTOR = 256
STARS = 4096
CAP = 256
CHUNK = 512
INNER = 8.0

F32 = jnp.float32
BF16 = jnp.bfloat16


def _split_np(table):
    high = np.asarray(table, np.float32).astype(jnp.bfloat16)
    low = (np.asarray(table, np.float64) - high.astype(np.float64)).astype(np.float32).astype(jnp.bfloat16)
    return high, low


def _sine():
    levels = np.arange(HEIGHTS) + 1
    turns = levels[:, None] * levels[None, :] % (2 * (HEIGHTS + 1))
    return math.sqrt(2.0 / (HEIGHTS + 1)) * np.sin(turns * (math.pi / (HEIGHTS + 1)))


def _trig():
    ids = np.arange(SECTOR)
    theta = (ids[:, None] * ids[None, :] % SECTOR) * (2.0 * math.pi / SECTOR)
    return np.cos(theta), np.sin(theta)


def _twist():
    residues = np.arange(8)
    angles = np.arange(AZIM)
    theta = (residues[:, None] * angles[None, :] % AZIM) * (2.0 * math.pi / AZIM)
    plus = np.cos(theta) + np.sin(theta)
    minus = np.cos(theta) - np.sin(theta)
    return plus.reshape(64, SECTOR).astype(np.float32), minus.reshape(64, SECTOR).astype(np.float32)


def _field_table():
    sine = _sine()
    shifted = np.zeros((HEIGHTS, HEIGHTS))
    shifted[:-1] += sine[1:]
    shifted[1:] -= sine[:-1]
    vertical = 0.5 * shifted
    table = np.zeros((4, HEIGHTS, 16, 3, 4))
    by_group = sine.reshape(HEIGHTS, 16, 4)
    table[0, :, :, 0, :] = by_group
    table[1, :, :, 1, :] = -by_group
    table[2, :, :, 2, :] = -by_group
    table[3, :, :, 0, :] = -vertical.reshape(HEIGHTS, 16, 4)
    return table.reshape(4 * HEIGHTS, 192) / AZIM


def _eigen():
    levels = np.arange(HEIGHTS) + 1.0
    return ((2.0 * np.sin(levels * (math.pi / (2 * (HEIGHTS + 1))))) ** 2).astype(np.float32)


def _row_of(radius):
    x, zh, y, c = radius >> 4, (radius >> 3) & 1, (radius >> 1) & 3, radius & 1
    return (((x * 4 + y) * 2 + c) * 2) + zh


def _split(value):
    high = value.astype(BF16)
    low = (value - high.astype(F32)).astype(BF16)
    return high, low


def _dot(a, b):
    return jnp.dot(a, b, preferred_element_type=F32)


def _dot3(a, b):
    (a_high, a_low), (b_high, b_low) = a, b
    return _dot(a_high, b_high) + (_dot(a_low, b_high) + _dot(a_high, b_low))


def _one_hot(ids, rows):
    lanes = ids.shape[1]
    here = lax.broadcasted_iota(jnp.int32, (rows, lanes), 0) == ids
    return jnp.where(here, 1.0, 0.0).astype(BF16)


def deposit_kernel(cells_ref, mass_ref, sine_high_ref, sine_low_ref, out_ref):
    total = jnp.zeros((HEIGHTS, SECTOR), F32)
    for start in range(0, STARS, CHUNK):
        cell = cells_ref[:, start : start + CHUNK]
        mass = mass_ref[:, start : start + CHUNK]
        layer = lax.shift_right_logical(cell, 8)
        angle = cell & 255
        here = lax.broadcasted_iota(jnp.int32, (HEIGHTS, CHUNK), 0) == layer
        left = jnp.where(here, mass, 0.0).astype(BF16)
        right = _one_hot(angle, SECTOR)
        total += lax.dot_general(
            left, right, (((1,), (1,)), ((), ())), preferred_element_type=F32
        )
    out_ref[...] = _dot3((sine_high_ref[...], sine_low_ref[...]), _split(total))


def forward_kernel(x_ref, plus_ref, minus_ref, high_ref, low_ref, out_ref):
    tiles = [x_ref[8 * a : 8 * a + 8, :] for a in range(8)]
    rows = []
    for n2 in range(8):
        even = tiles[0] * plus_ref[8 * n2 : 8 * n2 + 1, :]
        odd = tiles[0] * minus_ref[8 * n2 : 8 * n2 + 1, :]
        for a in range(1, 8):
            at = 8 * n2 + a
            even += tiles[a] * plus_ref[at : at + 1, :]
            odd += tiles[a] * minus_ref[at : at + 1, :]
        rows.append(jnp.concatenate([even, odd], axis=1))
    left = _split(jnp.concatenate(rows, axis=0))
    result = _dot3(left, (high_ref[...], low_ref[...]))
    for n2 in range(8):
        for k in range(4):
            for zh in range(2):
                at = n2 * 8 + zh * 4 + k
                spot = n2 * 8 + k * 2 + zh
                out_ref[spot : spot + 1, :] = result[at : at + 1, :]


def factor_kernel(eigen_ref, inverse_ref, carry_ref, factor_ref, joint_ref):
    group = lax.axis_index("az") * 2 + lax.axis_index("zh")
    place = (lax.axis_index("x") * 4 + lax.axis_index("y")) * 2 + lax.axis_index("c")
    level = group * 4 + lax.rem(place, 4)
    residue = lax.div(place, 4)
    eigen = eigen_ref[level]
    mode = lax.broadcasted_iota(jnp.int32, (1, SECTOR), 1) * 8 + residue
    mode = jnp.minimum(mode, AZIM - mode).astype(F32)
    square = mode * mode
    top = None
    bottom = None
    for step in range(RADII // 2):
        i = step
        radius = INNER + i + 0.5
        lower = -(radius - 0.5) / radius
        upper = -(radius + 0.5) / radius
        denom = (2.0 + eigen) + square * (1.0 / (radius * radius))
        if top is not None:
            denom = denom - lower * top
        inverse = 1.0 / denom
        top = upper * inverse
        row = _row_of(i)
        inverse_ref[row : row + 1, :] = -inverse
        carry_ref[row : row + 1, :] = -lower * inverse
        factor_ref[row : row + 1, :] = -top
        i = RADII - 1 - step
        radius = INNER + i + 0.5
        lower = -(radius - 0.5) / radius
        upper = -(radius + 0.5) / radius
        denom = (2.0 + eigen) + square * (1.0 / (radius * radius))
        if bottom is not None:
            denom = denom - upper * bottom
        inverse = 1.0 / denom
        bottom = lower * inverse
        row = _row_of(i)
        inverse_ref[row : row + 1, :] = -inverse
        carry_ref[row : row + 1, :] = -upper * inverse
        factor_ref[row : row + 1, :] = -bottom
    joint_ref[...] = jnp.broadcast_to(1.0 / (1.0 - top * bottom), (8, SECTOR))


def solve_kernel(source_ref, inverse_ref, carry_ref, factor_ref, joint_ref, out_ref, scaled_ref):
    half = RADII // 2
    scaled_ref[...] = source_ref[...] * inverse_ref[...]

    def at(ref, i):
        row = _row_of(i)
        return ref[row : row + 1, :]

    values = [None] * RADII
    values[0] = at(scaled_ref, 0)
    values[RADII - 1] = at(scaled_ref, RADII - 1)
    for step in range(1, half):
        i = step
        values[i] = at(scaled_ref, i) + at(carry_ref, i) * values[i - 1]
        i = RADII - 1 - step
        values[i] = at(scaled_ref, i) + at(carry_ref, i) * values[i + 1]
    solved = [None] * RADII
    solved[half - 1] = (values[half - 1] + at(factor_ref, half - 1) * values[half]) * joint_ref[0:1, :]
    solved[half] = values[half] + at(factor_ref, half) * solved[half - 1]
    for step in range(1, half):
        i = half - 1 - step
        solved[i] = values[i] + at(factor_ref, i) * solved[i + 1]
        i = half + step
        solved[i] = values[i] + at(factor_ref, i) * solved[i - 1]
    for i in range(RADII):
        row = _row_of(i)
        spot = (row >> 1) * 4 + (row & 1)
        out_ref[spot : spot + 1, :] = solved[i]
        if i == 0:
            slope = solved[1] * 0.5
        elif i == RADII - 1:
            slope = solved[RADII - 2] * -0.5
        else:
            slope = (solved[i + 1] - solved[i - 1]) * 0.5
        out_ref[spot + 2 : spot + 3, :] = slope


def inverse_kernel(x_ref, plus_ref, minus_ref, high_ref, low_ref, out_ref):
    fields = [[], [], []]
    for n2 in range(8):
        pair = []
        for field in range(2):
            spots = [n2 * 16 + k * 4 + field * 2 + zh for zh in range(2) for k in range(4)]
            pair.append(jnp.concatenate([x_ref[at : at + 1, :] for at in spots], axis=0))
        mode = lax.broadcasted_iota(jnp.int32, (8, SECTOR), 1) * 8 + n2
        signed = jnp.where(2 * mode < AZIM, mode, mode - AZIM)
        signed = jnp.where(2 * mode == AZIM, 0, signed).astype(F32)
        fields[0].append(pair[0])
        fields[1].append(pair[1])
        fields[2].append(pair[0] * signed)
    table = (high_ref[...], low_ref[...])
    for field in range(3):
        left = _split(jnp.concatenate(fields[field], axis=0))
        wave = _dot3(left, table)
        for a in range(8):
            total = None
            for n2 in range(8):
                even = wave[8 * n2 : 8 * n2 + 8, :SECTOR]
                odd = wave[8 * n2 : 8 * n2 + 8, SECTOR:]
                plus = plus_ref[8 * n2 + a : 8 * n2 + a + 1, :]
                minus = minus_ref[8 * n2 + a : 8 * n2 + a + 1, :]
                if field < 2:
                    term = even * plus + odd * minus
                else:
                    term = even * minus - odd * plus
                total = term if total is None else total + term
            for zh in range(2):
                spot = (a * 2 + zh) * 12 + field * 4
                out_ref[spot : spot + 4, :] = total[zh * 4 : zh * 4 + 4, :]


def pick_kernel(positions_ref, velocities_ref, mass_ref, cells_ref, active_ref, lists_ref, out_ref):
    wanted = jnp.concatenate([lists_ref[0:1, :], lists_ref[1:2, :]], axis=1)
    total = jnp.zeros((32, 2 * CAP), F32)
    for start in range(0, STARS, CHUNK):
        moving = jnp.concatenate(
            [positions_ref[:, start : start + CHUNK], velocities_ref[:, start : start + CHUNK]], axis=0
        )
        high = moving.astype(BF16).astype(F32)
        rest = moving - high
        middle = rest.astype(BF16).astype(F32)
        low = rest - middle
        cell = cells_ref[:, start : start + CHUNK]
        plain = jnp.concatenate(
            [
                mass_ref[:, start : start + CHUNK],
                lax.shift_right_logical(cell, 8).astype(F32),
                (cell & 255).astype(F32),
                active_ref[:, start : start + CHUNK].astype(F32),
                jnp.zeros((4, CHUNK), F32),
            ],
            axis=0,
        )
        pad = jnp.zeros((2, CHUNK), F32)
        left = jnp.concatenate([high, pad, middle, pad, low, pad, plain], axis=0).astype(BF16)
        ids = lax.broadcasted_iota(jnp.int32, (CHUNK, 2 * CAP), 0) + start
        hot = jnp.where(ids == wanted, 1.0, 0.0).astype(BF16)
        total += _dot(left, hot)
    out_ref[0:8, :] = (total[0:8] + total[8:16]) + total[16:24]
    out_ref[8:16, :] = total[24:32]


def _sample(fields, layer, angle):
    lanes = layer.shape[1]
    hot = _one_hot(angle, SECTOR)
    both = _dot(fields, hot)
    here = lax.broadcasted_iota(jnp.int32, (HEIGHTS, lanes), 0) == layer
    found = []
    for field in range(3):
        block = both[64 * field : 64 * field + 64] + both[192 + 64 * field : 256 + 64 * field]
        found.append(jnp.sum(jnp.where(here, block, 0.0), axis=0, keepdims=True))
    return found


def _advance(position, velocity, accel, live):
    radius = position[0]
    speed = [
        velocity[0] + live * accel[0],
        velocity[1] + live * (accel[1] / radius),
        velocity[2] + live * accel[2],
    ]
    place = [
        position[0] + live * speed[0],
        position[1] + live * (speed[1] / radius),
        position[2] + live * speed[2],
    ]
    return place + speed


def parcel_kernel(modes_ref, high_ref, low_ref, picked_ref, counts_ref, pot_ref, fields_ref, zero_ref, one_ref):
    result = _dot3((high_ref[...], low_ref[...]), _split(modes_ref[...]))
    pot_ref[...] = result[0:64]
    field_high, field_low = _split(result[64:256])
    fields = jnp.concatenate([field_high, field_low], axis=0)
    fields_ref[...] = fields
    picked = picked_ref[...]
    layer = picked[9:10].astype(jnp.int32)
    angle = picked[10:11].astype(jnp.int32)
    accel = _sample(fields, layer, angle)
    state = _advance(
        [picked[i : i + 1] for i in range(3)],
        [picked[i : i + 1] for i in range(3, 6)],
        accel,
        picked[11:12],
    )
    rows = jnp.concatenate(state + [picked[8:9]], axis=0)
    slots = lax.broadcasted_iota(jnp.int32, (7, CAP), 1)
    zero_ref[...] = jnp.where(slots < counts_ref[0:1, :], rows[:, :CAP], 0.0)
    one_ref[...] = jnp.where(slots < counts_ref[1:2, :], rows[:, CAP:], 0.0)


def stars_kernel(fields_ref, positions_ref, velocities_ref, cells_ref, active_ref, out_ref):
    fields = fields_ref[...]
    for start in range(0, STARS, CHUNK):
        lanes = slice(start, start + CHUNK)
        cell = cells_ref[:, lanes]
        accel = _sample(fields, lax.shift_right_logical(cell, 8), cell & 255)
        state = _advance(
            [positions_ref[i : i + 1, lanes] for i in range(3)],
            [velocities_ref[i : i + 1, lanes] for i in range(3)],
            accel,
            active_ref[:, lanes].astype(F32),
        )
        for row in range(6):
            out_ref[row : row + 1, lanes] = state[row]


def _call(kernel, out_shape, name, flops, in_smem=(), count=0, scratch=()):
    vmem = pl.BlockSpec(memory_space=pltpu.VMEM)
    smem = pl.BlockSpec(memory_space=pltpu.SMEM)
    outs = jax.tree.map(lambda _: vmem, out_shape)
    return pl.pallas_call(
        kernel,
        out_shape=out_shape,
        in_specs=[smem if i in in_smem else vmem for i in range(count)],
        out_specs=outs,
        scratch_shapes=list(scratch),
        name=name,
        cost_estimate=pl.CostEstimate(flops=flops, bytes_accessed=1 << 20, transcendentals=0),
        compiler_params=pltpu.CompilerParams(vmem_limit_bytes=48 << 20),
    )


def per_device(positions, velocities, masses, cells, active, send_lists, send_counts):
    shape = functools.partial(jax.ShapeDtypeStruct, dtype=F32)
    sine_high, sine_low = _split_np(_sine())
    cosine, sine = _trig()
    down_high, down_low = _split_np(np.concatenate([cosine, sine], axis=0))
    up_high, up_low = _split_np(np.concatenate([cosine, sine], axis=1))
    plus, minus = _twist()
    out_high, out_low = _split_np(_field_table())

    mass = masses.astype(F32).reshape(1, STARS)
    cell = cells.reshape(1, STARS)
    live = active.reshape(1, STARS)

    layered = _call(deposit_kernel, shape((64, SECTOR)), "deposit", 10**9, count=4)(
        cell, mass, sine_high, sine_low
    )
    sectors = lax.all_to_all(layered, ("az", "zh"), 0, 0, tiled=True)
    factors = _call(
        factor_kernel,
        (shape((64, SECTOR)), shape((64, SECTOR)), shape((64, SECTOR)), shape((8, SECTOR))),
        "factor",
        10**9,
        in_smem=(0,),
        count=1,
    )(_eigen())
    picked = _call(pick_kernel, shape((16, 2 * CAP)), "pick", 10**9, count=6)(
        positions, velocities, mass, cell, live, send_lists
    )
    spectrum = _call(forward_kernel, shape((64, SECTOR)), "forward", 10**9, count=5)(
        sectors, plus, minus, down_high, down_low
    )
    columns = lax.all_to_all(spectrum, ("x", "y", "c"), 0, 0, tiled=True)
    solved = _call(
        solve_kernel,
        shape((128, SECTOR)),
        "solve",
        10**9,
        count=5,
        scratch=[pltpu.VMEM((64, SECTOR), F32)],
    )(columns, *factors)
    waves = lax.all_to_all(solved, ("x", "y", "c"), 0, 0, tiled=True)
    angles = _call(inverse_kernel, shape((192, SECTOR)), "inverse", 10**9, count=5)(
        waves, plus, minus, up_high, up_low
    )
    modes = lax.all_to_all(angles, ("az", "zh"), 0, 0, tiled=True)
    potential, fields, zero, one = _call(
        parcel_kernel,
        (
            shape((64, SECTOR)),
            jax.ShapeDtypeStruct((384, SECTOR), BF16),
            shape((7, CAP)),
            shape((7, CAP)),
        ),
        "parcel",
        10**9,
        count=5,
    )(modes, out_high, out_low, picked, send_counts)
    from_lower = lax.ppermute(one, "az", [(i, (i + 1) % 8) for i in range(8)])
    from_upper = lax.ppermute(zero, "az", [((i + 1) % 8, i) for i in range(8)])
    state = _call(stars_kernel, shape((6, STARS)), "stars", 10**9, count=5)(
        fields, positions, velocities, cell, live
    )
    return potential.reshape(64, 1, SECTOR), state, jnp.stack([from_lower, from_upper])


def solution(mesh):
    fine = Mesh(mesh.devices.reshape(8, 4, 2, 4, 2), ("az", "x", "zh", "y", "c"))
    rz = ("x", "zh", "y", "c")
    every = ("az",) + rz
    return jax.shard_map(
        per_device,
        mesh=fine,
        in_specs=(
            P(None, every),
            P(None, every),
            P(every),
            P(every),
            P(every),
            P(None, every),
            P(None, every),
        ),
        out_specs=(P(None, rz, "az"), P(None, every), P(None, None, every)),
        check_vma=False,
    )
```

```python
import functools
import math

import jax
import jax.numpy as jnp
import numpy as np
from jax import lax
from jax.experimental import pallas as pl
from jax.experimental.pallas import tpu as pltpu
from jax.sharding import Mesh
from jax.sharding import PartitionSpec as P

HEIGHTS = 64
RADII = 64
AZIM = 2048
SECTOR = 256
STARS = 4096
CAP = 256
CHUNK = 512
INNER = 8.0

F32 = jnp.float32
BF16 = jnp.bfloat16


def _split_np(table):
    exact = np.asarray(table, np.float64)
    high = exact.astype(np.float32).astype(jnp.bfloat16)
    low = (exact - high.astype(np.float64)).astype(np.float32).astype(jnp.bfloat16)
    return np.concatenate([high, low], axis=0)


def _sine():
    levels = np.arange(HEIGHTS) + 1
    turns = levels[:, None] * levels[None, :] % (2 * (HEIGHTS + 1))
    return math.sqrt(2.0 / (HEIGHTS + 1)) * np.sin(turns * (math.pi / (HEIGHTS + 1)))


def _trig():
    ids = np.arange(SECTOR)
    theta = (ids[:, None] * ids[None, :] % SECTOR) * (2.0 * math.pi / SECTOR)
    return np.concatenate([np.cos(theta), np.sin(theta)], axis=0)


def _twist():
    residues = np.arange(8)
    angles = np.arange(AZIM)
    theta = (residues[:, None] * angles[None, :] % AZIM) * (2.0 * math.pi / AZIM)
    plus = np.cos(theta) + np.sin(theta)
    minus = np.cos(theta) - np.sin(theta)
    return np.concatenate([plus, minus], axis=0).reshape(128, SECTOR).astype(np.float32)


def _field_table():
    sine = _sine()
    shifted = np.zeros((HEIGHTS, HEIGHTS))
    shifted[:-1] += sine[1:]
    shifted[1:] -= sine[:-1]
    vertical = 0.5 * shifted
    table = np.zeros((4, HEIGHTS, 16, 3, 4))
    by_group = sine.reshape(HEIGHTS, 16, 4)
    table[0, :, :, 0, :] = by_group
    table[1, :, :, 1, :] = -by_group
    table[2, :, :, 2, :] = -by_group
    table[3, :, :, 0, :] = -vertical.reshape(HEIGHTS, 16, 4)
    return table.reshape(4 * HEIGHTS, 192) / AZIM


def _eigen():
    levels = np.arange(HEIGHTS) + 1.0
    return ((2.0 * np.sin(levels * (math.pi / (2 * (HEIGHTS + 1))))) ** 2).astype(np.float32)


def _row_of(radius):
    x, zh, y, c = radius >> 4, (radius >> 3) & 1, (radius >> 1) & 3, radius & 1
    return (((x * 4 + y) * 2 + c) * 2) + zh


def _split(value):
    high = value.astype(BF16)
    low = (value - high.astype(F32)).astype(BF16)
    return high, low


def _dot(a, b):
    return jnp.dot(a, b, preferred_element_type=F32)


def _dot3(a, b):
    (a_high, a_low), (b_high, b_low) = a, b
    return _dot(a_high, b_high) + (_dot(a_low, b_high) + _dot(a_high, b_low))


def _one_hot(ids, rows):
    lanes = ids.shape[1]
    here = lax.broadcasted_iota(jnp.int32, (rows, lanes), 0) == ids
    return jnp.where(here, 1.0, 0.0).astype(BF16)


def _sine_in_kernel():
    shape = (HEIGHTS, HEIGHTS)
    first = lax.broadcasted_iota(jnp.int32, shape, 0) + 1
    second = lax.broadcasted_iota(jnp.int32, shape, 1) + 1
    turns = lax.rem(first * second, 2 * (HEIGHTS + 1))
    negative = turns > HEIGHTS + 1
    turns = jnp.where(negative, turns - (HEIGHTS + 1), turns)
    turns = jnp.minimum(turns, HEIGHTS + 1 - turns).astype(F32)
    angle = turns * (math.pi / (HEIGHTS + 1))
    square = angle * angle
    series = jnp.full(shape, 1.0 / math.factorial(13), F32)
    for power in (11, 9, 7, 5, 3, 1):
        sign = -1.0 if power % 4 == 3 else 1.0
        series = series * square + sign / math.factorial(power)
    value = series * angle * math.sqrt(2.0 / (HEIGHTS + 1))
    return jnp.where(negative, -value, value)


def deposit_kernel(cells_hbm, mass_hbm, out_ref, cells_ref, mass_ref, sems):
    cells_copy = pltpu.make_async_copy(cells_hbm, cells_ref, sems.at[0])
    mass_copy = pltpu.make_async_copy(mass_hbm, mass_ref, sems.at[1])
    cells_copy.start()
    mass_copy.start()
    sine = _split(_sine_in_kernel())
    cells_copy.wait()
    mass_copy.wait()
    total = jnp.zeros((HEIGHTS, SECTOR), F32)
    for start in range(0, STARS, CHUNK):
        cell = cells_ref[:, start : start + CHUNK]
        mass = mass_ref[start : start + CHUNK].astype(F32).reshape(1, CHUNK)
        layer = lax.shift_right_logical(cell, 8)
        angle = cell & 255
        here = lax.broadcasted_iota(jnp.int32, (HEIGHTS, CHUNK), 0) == layer
        left = jnp.where(here, mass, 0.0).astype(BF16)
        right = _one_hot(angle, SECTOR)
        total += lax.dot_general(
            left, right, (((1,), (1,)), ((), ())), preferred_element_type=F32
        )
    layered = _dot3(sine, _split(total))
    for group in range(16):
        out_ref[group] = layered[4 * group : 4 * group + 4, :]


def forward_kernel(x_ref, twist_ref, table_ref, out_ref):
    tiles = []
    for a in range(8):
        tiles.append(jnp.concatenate([x_ref[2 * a], x_ref[2 * a + 1]], axis=0))
    rows = []
    for n2 in range(8):
        even = None
        odd = None
        for a in range(8):
            at = 8 * n2 + a
            plus = tiles[a] * twist_ref[at : at + 1, :]
            minus = tiles[a] * twist_ref[64 + at : 65 + at, :]
            even = plus if even is None else even + plus
            odd = minus if odd is None else odd + minus
        rows.append(jnp.concatenate([even, odd], axis=1))
    left = _split(jnp.concatenate(rows, axis=0))
    result = _dot3(left, (table_ref[0:512, :], table_ref[512:1024, :]))
    for n2 in range(8):
        for k in range(4):
            for zh in range(2):
                at = n2 * 8 + zh * 4 + k
                out_ref[n2 * 4 + k, zh : zh + 1, :] = result[at : at + 1, :]


def factor_kernel(eigen_ref, inverse_ref, carry_ref, factor_ref, joint_ref):
    group = lax.axis_index("az") * 2 + lax.axis_index("zh")
    place = (lax.axis_index("x") * 4 + lax.axis_index("y")) * 2 + lax.axis_index("c")
    level = group * 4 + lax.rem(place, 4)
    residue = lax.div(place, 4)
    eigen = eigen_ref[level]
    mode = lax.broadcasted_iota(jnp.int32, (1, SECTOR), 1) * 8 + residue
    mode = jnp.minimum(mode, AZIM - mode).astype(F32)
    square = mode * mode
    top = None
    bottom = None
    for step in range(RADII // 2):
        i = step
        radius = INNER + i + 0.5
        lower = -(radius - 0.5) / radius
        upper = -(radius + 0.5) / radius
        denom = (2.0 + eigen) + square * (1.0 / (radius * radius))
        if top is not None:
            denom = denom - lower * top
        inverse = 1.0 / denom
        top = upper * inverse
        row = _row_of(i)
        inverse_ref[row : row + 1, :] = -inverse
        carry_ref[row : row + 1, :] = -lower * inverse
        factor_ref[row : row + 1, :] = -top
        i = RADII - 1 - step
        radius = INNER + i + 0.5
        lower = -(radius - 0.5) / radius
        upper = -(radius + 0.5) / radius
        denom = (2.0 + eigen) + square * (1.0 / (radius * radius))
        if bottom is not None:
            denom = denom - upper * bottom
        inverse = 1.0 / denom
        bottom = lower * inverse
        row = _row_of(i)
        inverse_ref[row : row + 1, :] = -inverse
        carry_ref[row : row + 1, :] = -upper * inverse
        factor_ref[row : row + 1, :] = -bottom
    joint_ref[...] = jnp.broadcast_to(1.0 / (1.0 - top * bottom), (8, SECTOR))


def solve_kernel(source_ref, inverse_ref, carry_ref, factor_ref, joint_ref, out_ref, scaled_ref):
    half = RADII // 2
    for place in range(32):
        rows = slice(2 * place, 2 * place + 2)
        scaled_ref[rows, :] = source_ref[place] * inverse_ref[rows, :]

    def at(ref, i):
        row = _row_of(i)
        return ref[row : row + 1, :]

    values = [None] * RADII
    values[0] = at(scaled_ref, 0)
    values[RADII - 1] = at(scaled_ref, RADII - 1)
    for step in range(1, half):
        i = step
        values[i] = at(scaled_ref, i) + at(carry_ref, i) * values[i - 1]
        i = RADII - 1 - step
        values[i] = at(scaled_ref, i) + at(carry_ref, i) * values[i + 1]
    solved = [None] * RADII
    solved[half - 1] = (values[half - 1] + at(factor_ref, half - 1) * values[half]) * joint_ref[0:1, :]
    solved[half] = values[half] + at(factor_ref, half) * solved[half - 1]
    for step in range(1, half):
        i = half - 1 - step
        solved[i] = values[i] + at(factor_ref, i) * solved[i + 1]
        i = half + step
        solved[i] = values[i] + at(factor_ref, i) * solved[i - 1]
    for i in range(RADII):
        row = _row_of(i)
        place, zh = row >> 1, row & 1
        out_ref[place, zh : zh + 1, :] = solved[i]
        if i == 0:
            slope = solved[1] * 0.5
        elif i == RADII - 1:
            slope = solved[RADII - 2] * -0.5
        else:
            slope = (solved[i + 1] - solved[i - 1]) * 0.5
        out_ref[place, zh + 2 : zh + 3, :] = slope


def inverse_kernel(x_ref, twist_ref, table_ref, out_ref):
    fields = [[], [], []]
    for n2 in range(8):
        pair = []
        for field in range(2):
            spots = [(n2 * 4 + k, field * 2 + zh) for zh in range(2) for k in range(4)]
            pair.append(jnp.concatenate([x_ref[at, row : row + 1, :] for at, row in spots], axis=0))
        mode = lax.broadcasted_iota(jnp.int32, (8, SECTOR), 1) * 8 + n2
        signed = jnp.where(2 * mode < AZIM, mode, mode - AZIM)
        signed = jnp.where(2 * mode == AZIM, 0, signed).astype(F32)
        fields[0].append(pair[0])
        fields[1].append(pair[1])
        fields[2].append(pair[0] * signed)
    cosine = (table_ref[0:256, :], table_ref[512:768, :])
    sine = (table_ref[256:512, :], table_ref[768:1024, :])
    for field in range(3):
        left = _split(jnp.concatenate(fields[field], axis=0))
        evens = _dot3(left, cosine)
        odds = _dot3(left, sine)
        for a in range(8):
            total = None
            for n2 in range(8):
                even = evens[8 * n2 : 8 * n2 + 8, :]
                odd = odds[8 * n2 : 8 * n2 + 8, :]
                plus = twist_ref[8 * n2 + a : 8 * n2 + a + 1, :]
                minus = twist_ref[64 + 8 * n2 + a : 65 + 8 * n2 + a, :]
                if field < 2:
                    term = even * plus + odd * minus
                else:
                    term = even * minus - odd * plus
                total = term if total is None else total + term
            for zh in range(2):
                out_ref[a * 2 + zh, field] = total[zh * 4 : zh * 4 + 4, :]


def pick_kernel(positions_ref, velocities_ref, mass_ref, cells_ref, active_ref, lists_ref, counts_ref, out_ref):
    wanted = jnp.concatenate([lists_ref[0:1, :], lists_ref[1:2, :]], axis=1)
    total = jnp.zeros((32, 2 * CAP), F32)
    for start in range(0, STARS, CHUNK):
        moving = jnp.concatenate(
            [positions_ref[:, start : start + CHUNK], velocities_ref[:, start : start + CHUNK]], axis=0
        )
        high = moving.astype(BF16).astype(F32)
        rest = moving - high
        middle = rest.astype(BF16).astype(F32)
        low = rest - middle
        cell = cells_ref[:, start : start + CHUNK]
        plain = jnp.concatenate(
            [
                mass_ref[start : start + CHUNK].astype(F32).reshape(1, CHUNK),
                lax.shift_right_logical(cell, 8).astype(F32),
                (cell & 255).astype(F32),
                active_ref[:, start : start + CHUNK].astype(F32),
                jnp.zeros((4, CHUNK), F32),
            ],
            axis=0,
        )
        pad = jnp.zeros((2, CHUNK), F32)
        left = jnp.concatenate([high, pad, middle, pad, low, pad, plain], axis=0).astype(BF16)
        ids = lax.broadcasted_iota(jnp.int32, (CHUNK, 2 * CAP), 0) + start
        hot = jnp.where(ids == wanted, 1.0, 0.0).astype(BF16)
        total += _dot(left, hot)
    out_ref[0:8, :] = (total[0:8] + total[8:16]) + total[16:24]
    slots = lax.broadcasted_iota(jnp.int32, (1, CAP), 1)
    keep = [jnp.where(slots < counts_ref[:, i : i + 1], 1.0, 0.0) for i in range(2)]
    out_ref[8:12, :] = total[24:28]
    out_ref[12:13, :] = jnp.concatenate(keep, axis=1)


def _sample(fields, layer, angle):
    lanes = layer.shape[1]
    hot = _one_hot(angle, SECTOR)
    both = _dot(fields, hot)
    here = lax.broadcasted_iota(jnp.int32, (HEIGHTS, lanes), 0) == layer
    found = []
    for field in range(3):
        block = both[64 * field : 64 * field + 64] + both[192 + 64 * field : 256 + 64 * field]
        found.append(jnp.sum(jnp.where(here, block, 0.0), axis=0, keepdims=True))
    return found


def _advance(position, velocity, accel, live):
    radius = position[0]
    speed = [
        velocity[0] + live * accel[0],
        velocity[1] + live * (accel[1] / radius),
        velocity[2] + live * accel[2],
    ]
    place = [
        position[0] + live * speed[0],
        position[1] + live * (speed[1] / radius),
        position[2] + live * speed[2],
    ]
    return place + speed


def parcel_kernel(modes_ref, table_ref, picked_ref, pot_ref, fields_ref, wrap_ref, near_ref):
    modes = jnp.concatenate([modes_ref[group, field] for group in range(16) for field in range(3)], axis=0)
    result = _dot3((table_ref[0:256, :], table_ref[256:512, :]), _split(modes))
    pot_ref[...] = result[0:64]
    field_high, field_low = _split(result[64:256])
    fields = jnp.concatenate([field_high, field_low], axis=0)
    fields_ref[...] = fields
    picked = picked_ref[...]
    layer = picked[9:10].astype(jnp.int32)
    angle = picked[10:11].astype(jnp.int32)
    accel = _sample(fields, layer, angle)
    state = _advance(
        [picked[i : i + 1] for i in range(3)],
        [picked[i : i + 1] for i in range(3, 6)],
        accel,
        picked[11:12],
    )
    rows = jnp.concatenate(state + [picked[8:9]], axis=0)
    rows = jnp.where(picked[12:13] > 0.5, rows, 0.0)
    down = rows[:, :CAP]
    up = rows[:, CAP:]
    odd = lax.rem(lax.axis_index("az"), 2) == 1
    wrap_ref[...] = jnp.where(odd, up, down)
    near_ref[...] = jnp.where(odd, down, up)


def stars_kernel(pot_ref, fields_ref, positions_ref, velocities_ref, cells_ref, active_ref, grid_ref, out_ref):
    for h in range(HEIGHTS):
        grid_ref[h] = pot_ref[h : h + 1, :]
    fields = fields_ref[...]
    for start in range(0, STARS, CHUNK):
        lanes = slice(start, start + CHUNK)
        cell = cells_ref[:, lanes]
        accel = _sample(fields, lax.shift_right_logical(cell, 8), cell & 255)
        state = _advance(
            [positions_ref[i : i + 1, lanes] for i in range(3)],
            [velocities_ref[i : i + 1, lanes] for i in range(3)],
            accel,
            active_ref[:, lanes].astype(F32),
        )
        for row in range(6):
            out_ref[row : row + 1, lanes] = state[row]


def arrive_kernel(far_ref, close_ref, out_ref):
    odd = lax.rem(lax.axis_index("az"), 2) == 1
    far = far_ref[...]
    close = close_ref[...]
    lower = jnp.where(odd, close, far)
    upper = jnp.where(odd, far, close)
    for row in range(7):
        out_ref[row, 0:1, :] = lower[row : row + 1]
        out_ref[row, 1:2, :] = upper[row : row + 1]


def _call(kernel, out_shape, name, flops, in_smem=(), in_hbm=(), count=0, scratch=(), limit=48 << 20):
    vmem = pl.BlockSpec(memory_space=pltpu.VMEM)
    smem = pl.BlockSpec(memory_space=pltpu.SMEM)
    hbm = pl.BlockSpec(memory_space=pltpu.HBM)
    outs = jax.tree.map(lambda _: vmem, out_shape)
    return pl.pallas_call(
        kernel,
        out_shape=out_shape,
        in_specs=[smem if i in in_smem else hbm if i in in_hbm else vmem for i in range(count)],
        out_specs=outs,
        scratch_shapes=list(scratch),
        name=name,
        cost_estimate=pl.CostEstimate(flops=flops, bytes_accessed=1 << 20, transcendentals=0),
        compiler_params=pltpu.CompilerParams(vmem_limit_bytes=limit),
    )


def per_device(positions, velocities, masses, cells, active, send_lists, send_counts):
    shape = functools.partial(jax.ShapeDtypeStruct, dtype=F32)
    z_axes, plane_axes = ("az", "zh"), ("x", "y", "c")
    exchange = functools.partial(lax.all_to_all, split_axis=0, concat_axis=0, tiled=True)
    table = _split_np(_trig())
    twist = _twist()
    cell = cells.reshape(1, STARS)
    live = active.reshape(1, STARS)

    layered = _call(
        deposit_kernel,
        shape((16, 4, SECTOR)),
        "deposit",
        10**9,
        in_hbm=(0, 1),
        limit=None,
        count=2,
        scratch=[
            pltpu.VMEM((1, STARS), jnp.int32),
            pltpu.VMEM((STARS,), BF16),
            pltpu.SemaphoreType.DMA((2,)),
        ],
    )(cell, masses)
    sectors = exchange(layered, z_axes)
    spectrum = _call(forward_kernel, shape((32, 2, SECTOR)), "forward", 10**9, count=3)(
        sectors, twist, table
    )
    spectrum, eigen, send_lists = lax.optimization_barrier((spectrum, jnp.asarray(_eigen()), send_lists))
    columns = exchange(spectrum, plane_axes)
    factors = _call(
        factor_kernel,
        (shape((64, SECTOR)), shape((64, SECTOR)), shape((64, SECTOR)), shape((8, SECTOR))),
        "factor",
        10**9,
        in_smem=(0,),
        count=1,
    )(eigen)
    picked = _call(pick_kernel, shape((16, 2 * CAP)), "pick", 10**9, count=7)(
        positions, velocities, masses, cell, live, send_lists, send_counts.reshape(1, 2)
    )
    columns, factors, picked = lax.optimization_barrier((columns, factors, picked))
    solved = _call(
        solve_kernel,
        shape((32, 4, SECTOR)),
        "solve",
        10**9,
        count=5,
        scratch=[pltpu.VMEM((64, SECTOR), F32)],
    )(columns, *factors)
    waves = exchange(solved, plane_axes)
    angles = _call(inverse_kernel, shape((16, 3, 4, SECTOR)), "inverse", 10**9, count=3)(
        waves, twist, table
    )
    modes = exchange(angles, z_axes)
    grid, fields, wrap, near = _call(
        parcel_kernel,
        (
            shape((64, SECTOR)),
            jax.ShapeDtypeStruct((384, SECTOR), BF16),
            shape((7, CAP)),
            shape((7, CAP)),
        ),
        "parcel",
        10**9,
        count=3,
    )(modes, _split_np(_field_table()), picked)
    far = lax.ppermute(wrap, "az", [(i, (i + 1) % 8 if i % 2 else (i + 7) % 8) for i in range(8)])
    close = lax.ppermute(near, "az", [(i, i ^ 1) for i in range(8)])
    potential, state = _call(
        stars_kernel, (shape((64, 1, SECTOR)), shape((6, STARS))), "stars", 10**9, count=6
    )(grid, fields, positions, velocities, cell, live)
    arrivals = _call(arrive_kernel, shape((7, 2, CAP)), "arrive", 10**6, count=2)(far, close)
    return potential, state, arrivals.transpose(1, 0, 2)


def solution(mesh):
    fine = Mesh(mesh.devices.reshape(8, 4, 2, 4, 2), ("az", "x", "zh", "y", "c"))
    rz = ("x", "zh", "y", "c")
    every = ("az",) + rz
    return jax.shard_map(
        per_device,
        mesh=fine,
        in_specs=(
            P(None, every),
            P(None, every),
            P(every),
            P(every),
            P(every),
            P(None, every),
            P(None, every),
        ),
        out_specs=(P(None, rz, "az"), P(None, every), P(None, None, every)),
        check_vma=False,
    )
```

```python
import functools
import math

import jax
import jax.numpy as jnp
import numpy as np
from jax import lax
from jax.experimental import pallas as pl
from jax.experimental.pallas import tpu as pltpu
from jax.sharding import Mesh
from jax.sharding import PartitionSpec as P

HEIGHTS = 64
RADII = 64
AZIM = 2048
SECTOR = 256
STARS = 4096
CAP = 256
CHUNK = 512
INNER = 8.0

F32 = jnp.float32
BF16 = jnp.bfloat16


def _split_np(table):
    exact = np.asarray(table, np.float64)
    high = exact.astype(np.float32).astype(jnp.bfloat16)
    low = (exact - high.astype(np.float64)).astype(np.float32).astype(jnp.bfloat16)
    return np.concatenate([high, low], axis=0)


def _sine():
    levels = np.arange(HEIGHTS) + 1
    turns = levels[:, None] * levels[None, :] % (2 * (HEIGHTS + 1))
    return math.sqrt(2.0 / (HEIGHTS + 1)) * np.sin(turns * (math.pi / (HEIGHTS + 1)))


def _trig():
    ids = np.arange(SECTOR)
    theta = (ids[:, None] * ids[None, :] % SECTOR) * (2.0 * math.pi / SECTOR)
    return np.concatenate([np.cos(theta), np.sin(theta)], axis=0)


def _twist():
    residues = np.arange(8)
    angles = np.arange(AZIM)
    theta = (residues[:, None] * angles[None, :] % AZIM) * (2.0 * math.pi / AZIM)
    plus = np.cos(theta) + np.sin(theta)
    minus = np.cos(theta) - np.sin(theta)
    return np.concatenate([plus, minus], axis=0).reshape(128, SECTOR).astype(np.float32)


def _field_table():
    sine = _sine()
    shifted = np.zeros((HEIGHTS, HEIGHTS))
    shifted[:-1] += sine[1:]
    shifted[1:] -= sine[:-1]
    vertical = 0.5 * shifted
    table = np.zeros((4, HEIGHTS, 16, 3, 4))
    by_group = sine.reshape(HEIGHTS, 16, 4)
    table[0, :, :, 0, :] = by_group
    table[1, :, :, 1, :] = -by_group
    table[2, :, :, 2, :] = -by_group
    table[3, :, :, 0, :] = -vertical.reshape(HEIGHTS, 16, 4)
    return table.reshape(4 * HEIGHTS, 192) / AZIM


def _eigen():
    levels = np.arange(HEIGHTS) + 1.0
    return ((2.0 * np.sin(levels * (math.pi / (2 * (HEIGHTS + 1))))) ** 2).astype(np.float32)


def _row_of(radius):
    x, zh, y, c = radius >> 4, (radius >> 3) & 1, (radius >> 1) & 3, radius & 1
    return (((x * 4 + y) * 2 + c) * 2) + zh


def _split(value):
    high = value.astype(BF16)
    low = (value - high.astype(F32)).astype(BF16)
    return high, low


def _dot(a, b):
    return jnp.dot(a, b, preferred_element_type=F32)


def _dot3(a, b):
    (a_high, a_low), (b_high, b_low) = a, b
    return _dot(a_high, b_high) + (_dot(a_low, b_high) + _dot(a_high, b_low))


def _one_hot(ids, rows):
    lanes = ids.shape[1]
    here = lax.broadcasted_iota(jnp.int32, (rows, lanes), 0) == ids
    return jnp.where(here, 1.0, 0.0).astype(BF16)


def _sine_in_kernel():
    shape = (HEIGHTS, HEIGHTS)
    first = lax.broadcasted_iota(jnp.int32, shape, 0) + 1
    second = lax.broadcasted_iota(jnp.int32, shape, 1) + 1
    turns = lax.rem(first * second, 2 * (HEIGHTS + 1))
    negative = turns > HEIGHTS + 1
    turns = jnp.where(negative, turns - (HEIGHTS + 1), turns)
    turns = jnp.minimum(turns, HEIGHTS + 1 - turns).astype(F32)
    angle = turns * (math.pi / (HEIGHTS + 1))
    square = angle * angle
    series = jnp.full(shape, 1.0 / math.factorial(13), F32)
    for power in (11, 9, 7, 5, 3, 1):
        sign = -1.0 if power % 4 == 3 else 1.0
        series = series * square + sign / math.factorial(power)
    value = series * angle * math.sqrt(2.0 / (HEIGHTS + 1))
    return jnp.where(negative, -value, value)


def deposit_kernel(cells_hbm, mass_hbm, out_ref, cells_ref, mass_ref, sems):
    cells_copy = pltpu.make_async_copy(cells_hbm, cells_ref, sems.at[0])
    mass_copy = pltpu.make_async_copy(mass_hbm, mass_ref, sems.at[1])
    cells_copy.start()
    mass_copy.start()
    sine = _split(_sine_in_kernel())
    cells_copy.wait()
    mass_copy.wait()
    total = jnp.zeros((HEIGHTS, SECTOR), F32)
    for start in range(0, STARS, CHUNK):
        cell = cells_ref[:, start : start + CHUNK]
        mass = mass_ref[start : start + CHUNK].astype(F32).reshape(1, CHUNK)
        layer = lax.shift_right_logical(cell, 8)
        angle = cell & 255
        here = lax.broadcasted_iota(jnp.int32, (HEIGHTS, CHUNK), 0) == layer
        left = jnp.where(here, mass, 0.0).astype(BF16)
        right = _one_hot(angle, SECTOR)
        total += lax.dot_general(
            left, right, (((1,), (1,)), ((), ())), preferred_element_type=F32
        )
    layered = _dot3(sine, _split(total))
    for group in range(16):
        out_ref[group] = layered[4 * group : 4 * group + 4, :]


def forward_kernel(x_ref, twist_ref, table_ref, out_ref):
    tiles = []
    for a in range(8):
        tiles.append(jnp.concatenate([x_ref[2 * a], x_ref[2 * a + 1]], axis=0))
    rows = []
    for n2 in range(8):
        even = None
        odd = None
        for a in range(8):
            at = 8 * n2 + a
            plus = tiles[a] * twist_ref[at : at + 1, :]
            minus = tiles[a] * twist_ref[64 + at : 65 + at, :]
            even = plus if even is None else even + plus
            odd = minus if odd is None else odd + minus
        rows.append(jnp.concatenate([even, odd], axis=1))
    left = _split(jnp.concatenate(rows, axis=0))
    result = _dot3(left, (table_ref[0:512, :], table_ref[512:1024, :]))
    for n2 in range(8):
        for k in range(4):
            for zh in range(2):
                at = n2 * 8 + zh * 4 + k
                out_ref[n2 * 4 + k, zh : zh + 1, :] = result[at : at + 1, :]


def factor_kernel(eigen_ref, inverse_ref, carry_ref, factor_ref, joint_ref):
    group = lax.axis_index("az") * 2 + lax.axis_index("zh")
    place = (lax.axis_index("x") * 4 + lax.axis_index("y")) * 2 + lax.axis_index("c")
    level = group * 4 + lax.rem(place, 4)
    residue = lax.div(place, 4)
    eigen = eigen_ref[level]
    mode = lax.broadcasted_iota(jnp.int32, (1, SECTOR), 1) * 8 + residue
    mode = jnp.minimum(mode, AZIM - mode).astype(F32)
    square = mode * mode
    top = None
    bottom = None
    for step in range(RADII // 2):
        i = step
        radius = INNER + i + 0.5
        lower = -(radius - 0.5) / radius
        upper = -(radius + 0.5) / radius
        denom = (2.0 + eigen) + square * (1.0 / (radius * radius))
        if top is not None:
            denom = denom - lower * top
        inverse = 1.0 / denom
        top = upper * inverse
        row = _row_of(i)
        inverse_ref[row : row + 1, :] = -inverse
        carry_ref[row : row + 1, :] = -lower * inverse
        factor_ref[row : row + 1, :] = -top
        i = RADII - 1 - step
        radius = INNER + i + 0.5
        lower = -(radius - 0.5) / radius
        upper = -(radius + 0.5) / radius
        denom = (2.0 + eigen) + square * (1.0 / (radius * radius))
        if bottom is not None:
            denom = denom - upper * bottom
        inverse = 1.0 / denom
        bottom = lower * inverse
        row = _row_of(i)
        inverse_ref[row : row + 1, :] = -inverse
        carry_ref[row : row + 1, :] = -upper * inverse
        factor_ref[row : row + 1, :] = -bottom
    joint_ref[...] = jnp.broadcast_to(1.0 / (1.0 - top * bottom), (8, SECTOR))


def solve_kernel(source_ref, inverse_ref, carry_ref, factor_ref, joint_ref, out_ref, scaled_ref):
    half = RADII // 2
    for place in range(32):
        rows = slice(2 * place, 2 * place + 2)
        scaled_ref[rows, :] = source_ref[place] * inverse_ref[rows, :]

    def at(ref, i):
        row = _row_of(i)
        return ref[row : row + 1, :]

    values = [None] * RADII
    values[0] = at(scaled_ref, 0)
    values[RADII - 1] = at(scaled_ref, RADII - 1)
    for step in range(1, half):
        i = step
        values[i] = at(scaled_ref, i) + at(carry_ref, i) * values[i - 1]
        i = RADII - 1 - step
        values[i] = at(scaled_ref, i) + at(carry_ref, i) * values[i + 1]
    solved = [None] * RADII
    solved[half - 1] = (values[half - 1] + at(factor_ref, half - 1) * values[half]) * joint_ref[0:1, :]
    solved[half] = values[half] + at(factor_ref, half) * solved[half - 1]
    for step in range(1, half):
        i = half - 1 - step
        solved[i] = values[i] + at(factor_ref, i) * solved[i + 1]
        i = half + step
        solved[i] = values[i] + at(factor_ref, i) * solved[i - 1]
    for i in range(RADII):
        row = _row_of(i)
        place, zh = row >> 1, row & 1
        out_ref[place, zh : zh + 1, :] = solved[i]
        if i == 0:
            slope = solved[1] * 0.5
        elif i == RADII - 1:
            slope = solved[RADII - 2] * -0.5
        else:
            slope = (solved[i + 1] - solved[i - 1]) * 0.5
        out_ref[place, zh + 2 : zh + 3, :] = slope


def inverse_kernel(x_ref, twist_ref, table_ref, out_ref):
    fields = [[], [], []]
    for n2 in range(8):
        pair = []
        for field in range(2):
            spots = [(n2 * 4 + k, field * 2 + zh) for zh in range(2) for k in range(4)]
            pair.append(jnp.concatenate([x_ref[at, row : row + 1, :] for at, row in spots], axis=0))
        mode = lax.broadcasted_iota(jnp.int32, (8, SECTOR), 1) * 8 + n2
        signed = jnp.where(2 * mode < AZIM, mode, mode - AZIM)
        signed = jnp.where(2 * mode == AZIM, 0, signed).astype(F32)
        fields[0].append(pair[0])
        fields[1].append(pair[1])
        fields[2].append(pair[0] * signed)
    cosine = (table_ref[0:256, :], table_ref[512:768, :])
    sine = (table_ref[256:512, :], table_ref[768:1024, :])
    for field in range(3):
        left = _split(jnp.concatenate(fields[field], axis=0))
        evens = _dot3(left, cosine)
        odds = _dot3(left, sine)
        for a in range(8):
            total = None
            for n2 in range(8):
                even = evens[8 * n2 : 8 * n2 + 8, :]
                odd = odds[8 * n2 : 8 * n2 + 8, :]
                plus = twist_ref[8 * n2 + a : 8 * n2 + a + 1, :]
                minus = twist_ref[64 + 8 * n2 + a : 65 + 8 * n2 + a, :]
                if field < 2:
                    term = even * plus + odd * minus
                else:
                    term = even * minus - odd * plus
                total = term if total is None else total + term
            for zh in range(2):
                out_ref[a * 2 + zh, field] = total[zh * 4 : zh * 4 + 4, :]


def pick_kernel(positions_ref, velocities_ref, mass_ref, cells_ref, active_ref, lists_ref, counts_ref, out_ref):
    wanted = jnp.concatenate([lists_ref[0:1, :], lists_ref[1:2, :]], axis=1)
    total = jnp.zeros((32, 2 * CAP), F32)
    for start in range(0, STARS, CHUNK):
        moving = jnp.concatenate(
            [positions_ref[:, start : start + CHUNK], velocities_ref[:, start : start + CHUNK]], axis=0
        )
        high = moving.astype(BF16).astype(F32)
        rest = moving - high
        middle = rest.astype(BF16).astype(F32)
        low = rest - middle
        cell = cells_ref[:, start : start + CHUNK]
        plain = jnp.concatenate(
            [
                mass_ref[start : start + CHUNK].astype(F32).reshape(1, CHUNK),
                lax.shift_right_logical(cell, 8).astype(F32),
                (cell & 255).astype(F32),
                active_ref[:, start : start + CHUNK].astype(F32),
                jnp.zeros((4, CHUNK), F32),
            ],
            axis=0,
        )
        pad = jnp.zeros((2, CHUNK), F32)
        left = jnp.concatenate([high, pad, middle, pad, low, pad, plain], axis=0).astype(BF16)
        ids = lax.broadcasted_iota(jnp.int32, (CHUNK, 2 * CAP), 0) + start
        hot = jnp.where(ids == wanted, 1.0, 0.0).astype(BF16)
        total += _dot(left, hot)
    out_ref[0:8, :] = (total[0:8] + total[8:16]) + total[16:24]
    slots = lax.broadcasted_iota(jnp.int32, (1, CAP), 1)
    keep = [jnp.where(slots < counts_ref[:, i : i + 1], 1.0, 0.0) for i in range(2)]
    out_ref[8:12, :] = total[24:28]
    out_ref[12:13, :] = jnp.concatenate(keep, axis=1)


def _sample(fields, layer, angle):
    lanes = layer.shape[1]
    hot = _one_hot(angle, SECTOR)
    both = _dot(fields, hot)
    here = lax.broadcasted_iota(jnp.int32, (HEIGHTS, lanes), 0) == layer
    found = []
    for field in range(3):
        block = both[64 * field : 64 * field + 64] + both[192 + 64 * field : 256 + 64 * field]
        found.append(jnp.sum(jnp.where(here, block, 0.0), axis=0, keepdims=True))
    return found


def _advance(position, velocity, accel, live):
    radius = position[0]
    speed = [
        velocity[0] + live * accel[0],
        velocity[1] + live * (accel[1] / radius),
        velocity[2] + live * accel[2],
    ]
    place = [
        position[0] + live * speed[0],
        position[1] + live * (speed[1] / radius),
        position[2] + live * speed[2],
    ]
    return place + speed


def parcel_kernel(modes_ref, table_ref, picked_ref, pot_ref, fields_ref, wrap_ref, near_ref):
    modes = jnp.concatenate([modes_ref[group, field] for group in range(16) for field in range(3)], axis=0)
    result = _dot3((table_ref[0:256, :], table_ref[256:512, :]), _split(modes))
    pot_ref[...] = result[0:64]
    field_high, field_low = _split(result[64:256])
    fields = jnp.concatenate([field_high, field_low], axis=0)
    fields_ref[...] = fields
    picked = picked_ref[...]
    layer = picked[9:10].astype(jnp.int32)
    angle = picked[10:11].astype(jnp.int32)
    accel = _sample(fields, layer, angle)
    state = _advance(
        [picked[i : i + 1] for i in range(3)],
        [picked[i : i + 1] for i in range(3, 6)],
        accel,
        picked[11:12],
    )
    rows = jnp.concatenate(state + [picked[8:9]], axis=0)
    rows = jnp.where(picked[12:13] > 0.5, rows, 0.0)
    down = rows[:, :CAP]
    up = rows[:, CAP:]
    odd = lax.rem(lax.axis_index("az"), 2) == 1
    wrap_ref[...] = jnp.where(odd, up, down)
    near_ref[...] = jnp.where(odd, down, up)


def stars_kernel(pot_ref, fields_ref, positions_ref, velocities_ref, cells_ref, active_ref, grid_ref, out_ref):
    for h in range(HEIGHTS):
        grid_ref[h] = pot_ref[h : h + 1, :]
    fields = fields_ref[...]
    for start in range(0, STARS, CHUNK):
        lanes = slice(start, start + CHUNK)
        cell = cells_ref[:, lanes]
        accel = _sample(fields, lax.shift_right_logical(cell, 8), cell & 255)
        state = _advance(
            [positions_ref[i : i + 1, lanes] for i in range(3)],
            [velocities_ref[i : i + 1, lanes] for i in range(3)],
            accel,
            active_ref[:, lanes].astype(F32),
        )
        for row in range(6):
            out_ref[row : row + 1, lanes] = state[row]


def arrive_kernel(far_ref, close_ref, out_ref):
    odd = lax.rem(lax.axis_index("az"), 2) == 1
    far = far_ref[...]
    close = close_ref[...]
    lower = jnp.where(odd, close, far)
    upper = jnp.where(odd, far, close)
    for row in range(7):
        out_ref[row, 0:1, :] = lower[row : row + 1]
        out_ref[row, 1:2, :] = upper[row : row + 1]


def _call(kernel, out_shape, name, flops, in_smem=(), in_hbm=(), count=0, scratch=(), limit=48 << 20):
    vmem = pl.BlockSpec(memory_space=pltpu.VMEM)
    smem = pl.BlockSpec(memory_space=pltpu.SMEM)
    hbm = pl.BlockSpec(memory_space=pltpu.HBM)
    outs = jax.tree.map(lambda _: vmem, out_shape)
    return pl.pallas_call(
        kernel,
        out_shape=out_shape,
        in_specs=[smem if i in in_smem else hbm if i in in_hbm else vmem for i in range(count)],
        out_specs=outs,
        scratch_shapes=list(scratch),
        name=name,
        cost_estimate=pl.CostEstimate(flops=flops, bytes_accessed=1 << 20, transcendentals=0),
        compiler_params=pltpu.CompilerParams(vmem_limit_bytes=limit),
    )


def per_device(positions, velocities, masses, cells, active, send_lists, send_counts):
    shape = functools.partial(jax.ShapeDtypeStruct, dtype=F32)
    z_axes, plane_axes = ("az", "zh"), ("x", "y", "c")
    exchange = functools.partial(lax.all_to_all, split_axis=0, concat_axis=0, tiled=True)
    table = _split_np(_trig())
    twist = _twist()
    cell = cells.reshape(1, STARS)
    live = active.reshape(1, STARS)

    layered = _call(
        deposit_kernel,
        shape((16, 4, SECTOR)),
        "deposit",
        10**9,
        in_hbm=(0, 1),
        limit=None,
        count=2,
        scratch=[
            pltpu.VMEM((1, STARS), jnp.int32),
            pltpu.VMEM((STARS,), BF16),
            pltpu.SemaphoreType.DMA((2,)),
        ],
    )(cell, masses)
    layered, eigen, send_lists = lax.optimization_barrier((layered, jnp.asarray(_eigen()), send_lists))
    sectors = exchange(layered, z_axes)
    factors = _call(
        factor_kernel,
        (shape((64, SECTOR)), shape((64, SECTOR)), shape((64, SECTOR)), shape((8, SECTOR))),
        "factor",
        10**9,
        in_smem=(0,),
        count=1,
    )(eigen)
    picked = _call(pick_kernel, shape((16, 2 * CAP)), "pick", 10**9, count=7)(
        positions, velocities, masses, cell, live, send_lists, send_counts.reshape(1, 2)
    )
    sectors, factors, picked = lax.optimization_barrier((sectors, factors, picked))
    spectrum = _call(forward_kernel, shape((32, 2, SECTOR)), "forward", 10**9, count=3)(
        sectors, twist, table
    )
    columns = exchange(spectrum, plane_axes)
    solved = _call(
        solve_kernel,
        shape((32, 4, SECTOR)),
        "solve",
        10**9,
        count=5,
        scratch=[pltpu.VMEM((64, SECTOR), F32)],
    )(columns, *factors)
    waves = exchange(solved, plane_axes)
    angles = _call(inverse_kernel, shape((16, 3, 4, SECTOR)), "inverse", 10**9, count=3)(
        waves, twist, table
    )
    modes = exchange(angles, z_axes)
    grid, fields, wrap, near = _call(
        parcel_kernel,
        (
            shape((64, SECTOR)),
            jax.ShapeDtypeStruct((384, SECTOR), BF16),
            shape((7, CAP)),
            shape((7, CAP)),
        ),
        "parcel",
        10**9,
        count=3,
    )(modes, _split_np(_field_table()), picked)
    far = lax.ppermute(wrap, "az", [(i, (i + 1) % 8 if i % 2 else (i + 7) % 8) for i in range(8)])
    close = lax.ppermute(near, "az", [(i, i ^ 1) for i in range(8)])
    potential, state = _call(
        stars_kernel, (shape((64, 1, SECTOR)), shape((6, STARS))), "stars", 10**9, count=6
    )(grid, fields, positions, velocities, cell, live)
    arrivals = _call(arrive_kernel, shape((7, 2, CAP)), "arrive", 10**6, count=2)(far, close)
    return potential, state, arrivals.transpose(1, 0, 2)


def solution(mesh):
    fine = Mesh(mesh.devices.reshape(8, 4, 2, 4, 2), ("az", "x", "zh", "y", "c"))
    rz = ("x", "zh", "y", "c")
    every = ("az",) + rz
    return jax.shard_map(
        per_device,
        mesh=fine,
        in_specs=(
            P(None, every),
            P(None, every),
            P(every),
            P(every),
            P(every),
            P(None, every),
            P(None, every),
        ),
        out_specs=(P(None, rz, "az"), P(None, every), P(None, None, every)),
        check_vma=False,
    )
```

```python
import functools
import math

import jax
import jax.numpy as jnp
import numpy as np
from jax import lax
from jax.experimental import pallas as pl
from jax.experimental.pallas import tpu as pltpu
from jax.sharding import Mesh
from jax.sharding import PartitionSpec as P

HEIGHTS = 64
RADII = 64
AZIM = 2048
SECTOR = 256
STARS = 4096
CAP = 256
CHUNK = 512
INNER = 8.0

F32 = jnp.float32
BF16 = jnp.bfloat16


def _split_np(table):
    exact = np.asarray(table, np.float64)
    high = exact.astype(np.float32).astype(jnp.bfloat16)
    low = (exact - high.astype(np.float64)).astype(np.float32).astype(jnp.bfloat16)
    return np.concatenate([high, low], axis=0)


def _sine():
    levels = np.arange(HEIGHTS) + 1
    turns = levels[:, None] * levels[None, :] % (2 * (HEIGHTS + 1))
    return math.sqrt(2.0 / (HEIGHTS + 1)) * np.sin(turns * (math.pi / (HEIGHTS + 1)))


def _trig():
    ids = np.arange(SECTOR)
    theta = (ids[:, None] * ids[None, :] % SECTOR) * (2.0 * math.pi / SECTOR)
    return np.concatenate([np.cos(theta), np.sin(theta)], axis=0)


def _twist():
    residues = np.arange(8)
    angles = np.arange(AZIM)
    theta = (residues[:, None] * angles[None, :] % AZIM) * (2.0 * math.pi / AZIM)
    plus = np.cos(theta) + np.sin(theta)
    minus = np.cos(theta) - np.sin(theta)
    return np.concatenate([plus, minus], axis=0).reshape(128, SECTOR).astype(np.float32)


def _field_table():
    sine = _sine()
    shifted = np.zeros((HEIGHTS, HEIGHTS))
    shifted[:-1] += sine[1:]
    shifted[1:] -= sine[:-1]
    vertical = 0.5 * shifted
    table = np.zeros((4, HEIGHTS, 16, 3, 4))
    by_group = sine.reshape(HEIGHTS, 16, 4)
    table[0, :, :, 0, :] = by_group
    table[1, :, :, 1, :] = -by_group
    table[2, :, :, 2, :] = -by_group
    table[3, :, :, 0, :] = -vertical.reshape(HEIGHTS, 16, 4)
    return table.reshape(4 * HEIGHTS, 192) / AZIM


def _weight_table():
    table = _field_table().reshape(4, HEIGHTS, 16, 3, 4)
    sine = table[1, :, :, 1, :]
    vertical = table[3, :, :, 0, :]
    exact = np.zeros((16, 2, 2, 2, 4, HEIGHTS))
    for zh in range(2):
        exact[:, zh, 0, zh] = sine.transpose(1, 2, 0)
        exact[:, zh, 1, zh] = vertical.transpose(1, 2, 0)
    exact = exact.reshape(16 * 2 * 16, HEIGHTS)
    both = _split_np(exact).reshape(2, 16, 2, 16, HEIGHTS)
    return both.transpose(1, 2, 0, 3, 4).reshape(16, 2, 32, HEIGHTS)


def _eigen():
    levels = np.arange(HEIGHTS) + 1.0
    return ((2.0 * np.sin(levels * (math.pi / (2 * (HEIGHTS + 1))))) ** 2).astype(np.float32)


def _row_of(radius):
    x, zh, y, c = radius >> 4, (radius >> 3) & 1, (radius >> 1) & 3, radius & 1
    return (((x * 4 + y) * 2 + c) * 2) + zh


def _split(value):
    high = value.astype(BF16)
    low = (value - high.astype(F32)).astype(BF16)
    return high, low


def _dot(a, b):
    return jnp.dot(a, b, preferred_element_type=F32)


def _dot3(a, b):
    (a_high, a_low), (b_high, b_low) = a, b
    return _dot(a_high, b_high) + (_dot(a_low, b_high) + _dot(a_high, b_low))


def _one_hot(ids, rows):
    lanes = ids.shape[1]
    here = lax.broadcasted_iota(jnp.int32, (rows, lanes), 0) == ids
    return jnp.where(here, 1.0, 0.0).astype(BF16)


def _sine_in_kernel():
    shape = (HEIGHTS, HEIGHTS)
    first = lax.broadcasted_iota(jnp.int32, shape, 0) + 1
    second = lax.broadcasted_iota(jnp.int32, shape, 1) + 1
    turns = lax.rem(first * second, 2 * (HEIGHTS + 1))
    negative = turns > HEIGHTS + 1
    turns = jnp.where(negative, turns - (HEIGHTS + 1), turns)
    turns = jnp.minimum(turns, HEIGHTS + 1 - turns).astype(F32)
    angle = turns * (math.pi / (HEIGHTS + 1))
    square = angle * angle
    series = jnp.full(shape, 1.0 / math.factorial(13), F32)
    for power in (11, 9, 7, 5, 3, 1):
        sign = -1.0 if power % 4 == 3 else 1.0
        series = series * square + sign / math.factorial(power)
    value = series * angle * math.sqrt(2.0 / (HEIGHTS + 1))
    return jnp.where(negative, -value, value)


def deposit_kernel(cells_hbm, mass_hbm, lists_hbm, out_ref, cells_ref, mass_ref, lists_ref, sems):
    cells_copy = pltpu.make_async_copy(cells_hbm, cells_ref, sems.at[0])
    mass_copy = pltpu.make_async_copy(mass_hbm, mass_ref, sems.at[1])
    lists_copy = pltpu.make_async_copy(lists_hbm, lists_ref, sems.at[2])
    cells_copy.start()
    lists_copy.start()
    mass_copy.start()
    sine = _split(_sine_in_kernel())
    cells_copy.wait()
    lists_copy.wait()
    mass_copy.wait()
    wanted = jnp.concatenate([lists_ref[0:1, :], lists_ref[1:2, :]], axis=1)
    sent = jnp.zeros((16, 2 * CAP), F32)
    total = jnp.zeros((HEIGHTS, SECTOR), F32)
    for start in range(0, STARS, CHUNK):
        cell = cells_ref[:, start : start + CHUNK]
        mass = mass_ref[start : start + CHUNK].astype(F32).reshape(1, CHUNK)
        layer = lax.shift_right_logical(cell, 8)
        angle = cell & 255
        pair = jnp.concatenate([layer, angle, jnp.zeros((14, CHUNK), jnp.int32)], axis=0)
        ids = lax.broadcasted_iota(jnp.int32, (CHUNK, 2 * CAP), 0) + start
        hot = jnp.where(ids == wanted, 1.0, 0.0).astype(BF16)
        sent += _dot(pair.astype(F32).astype(BF16), hot)
        here = lax.broadcasted_iota(jnp.int32, (HEIGHTS, CHUNK), 0) == layer
        left = jnp.where(here, mass, 0.0).astype(BF16)
        right = _one_hot(angle, SECTOR)
        total += lax.dot_general(
            left, right, (((1,), (1,)), ((), ())), preferred_element_type=F32
        )
    layered = _dot3(sine, _split(total))
    sent_cell = sent[0:1] * 256.0 + sent[1:2]
    for group in range(16):
        out_ref[group, 0] = layered[4 * group : 4 * group + 2, :]
        out_ref[group, 1] = layered[4 * group + 2 : 4 * group + 4, :]
        out_ref[group, 2, 0:1, :] = sent_cell[:, :CAP]
        out_ref[group, 2, 1:2, :] = sent_cell[:, CAP:]


def forward_kernel(x_ref, twist_ref, table_ref, out_ref):
    tiles = []
    for a in range(8):
        parts = [x_ref[2 * a + zh, half] for zh in range(2) for half in range(2)]
        tiles.append(jnp.concatenate(parts, axis=0))
    rows = []
    for n2 in range(8):
        even = None
        odd = None
        for a in range(8):
            at = 8 * n2 + a
            plus = tiles[a] * twist_ref[at : at + 1, :]
            minus = tiles[a] * twist_ref[64 + at : 65 + at, :]
            even = plus if even is None else even + plus
            odd = minus if odd is None else odd + minus
        rows.append(jnp.concatenate([even, odd], axis=1))
    left = _split(jnp.concatenate(rows, axis=0))
    result = _dot3(left, (table_ref[0:512, :], table_ref[512:1024, :]))
    for n2 in range(8):
        for k in range(4):
            for zh in range(2):
                at = n2 * 8 + zh * 4 + k
                out_ref[n2 * 4 + k, zh : zh + 1, :] = result[at : at + 1, :]


def factor_kernel(eigen_ref, inverse_ref, carry_ref, factor_ref, joint_ref):
    group = lax.axis_index("az") * 2 + lax.axis_index("zh")
    place = (lax.axis_index("x") * 4 + lax.axis_index("y")) * 2 + lax.axis_index("c")
    level = group * 4 + lax.rem(place, 4)
    residue = lax.div(place, 4)
    eigen = eigen_ref[level]
    mode = lax.broadcasted_iota(jnp.int32, (1, SECTOR), 1) * 8 + residue
    mode = jnp.minimum(mode, AZIM - mode).astype(F32)
    square = mode * mode
    top = None
    bottom = None
    for step in range(RADII // 2):
        i = step
        radius = INNER + i + 0.5
        lower = -(radius - 0.5) / radius
        upper = -(radius + 0.5) / radius
        denom = (2.0 + eigen) + square * (1.0 / (radius * radius))
        if top is not None:
            denom = denom - lower * top
        inverse = 1.0 / denom
        top = upper * inverse
        row = _row_of(i)
        inverse_ref[row : row + 1, :] = -inverse
        carry_ref[row : row + 1, :] = -lower * inverse
        factor_ref[row : row + 1, :] = -top
        i = RADII - 1 - step
        radius = INNER + i + 0.5
        lower = -(radius - 0.5) / radius
        upper = -(radius + 0.5) / radius
        denom = (2.0 + eigen) + square * (1.0 / (radius * radius))
        if bottom is not None:
            denom = denom - upper * bottom
        inverse = 1.0 / denom
        bottom = lower * inverse
        row = _row_of(i)
        inverse_ref[row : row + 1, :] = -inverse
        carry_ref[row : row + 1, :] = -upper * inverse
        factor_ref[row : row + 1, :] = -bottom
    joint_ref[...] = jnp.broadcast_to(1.0 / (1.0 - top * bottom), (8, SECTOR))


def solve_kernel(source_ref, inverse_ref, carry_ref, factor_ref, joint_ref, out_ref, scaled_ref):
    half = RADII // 2
    for place in range(32):
        rows = slice(2 * place, 2 * place + 2)
        scaled_ref[rows, :] = source_ref[place] * inverse_ref[rows, :]

    def at(ref, i):
        row = _row_of(i)
        return ref[row : row + 1, :]

    values = [None] * RADII
    values[0] = at(scaled_ref, 0)
    values[RADII - 1] = at(scaled_ref, RADII - 1)
    for step in range(1, half):
        i = step
        values[i] = at(scaled_ref, i) + at(carry_ref, i) * values[i - 1]
        i = RADII - 1 - step
        values[i] = at(scaled_ref, i) + at(carry_ref, i) * values[i + 1]
    solved = [None] * RADII
    solved[half - 1] = (values[half - 1] + at(factor_ref, half - 1) * values[half]) * joint_ref[0:1, :]
    solved[half] = values[half] + at(factor_ref, half) * solved[half - 1]
    for step in range(1, half):
        i = half - 1 - step
        solved[i] = values[i] + at(factor_ref, i) * solved[i + 1]
        i = half + step
        solved[i] = values[i] + at(factor_ref, i) * solved[i - 1]
    for i in range(RADII):
        row = _row_of(i)
        place, zh = row >> 1, row & 1
        out_ref[place, zh : zh + 1, :] = solved[i]
        if i == 0:
            slope = solved[1] * 0.5
        elif i == RADII - 1:
            slope = solved[RADII - 2] * -0.5
        else:
            slope = (solved[i + 1] - solved[i - 1]) * 0.5
        out_ref[place, zh + 2 : zh + 3, :] = slope


def inverse_kernel(x_ref, twist_ref, table_ref, cells_ref, weight_ref, out_ref):
    group = lax.axis_index("az") * 2 + lax.axis_index("zh")
    fields = [[], [], []]
    for n2 in range(8):
        pair = []
        for field in range(2):
            spots = [(n2 * 4 + k, field * 2 + zh) for zh in range(2) for k in range(4)]
            pair.append(jnp.concatenate([x_ref[at, row : row + 1, :] for at, row in spots], axis=0))
        mode = lax.broadcasted_iota(jnp.int32, (8, SECTOR), 1) * 8 + n2
        signed = jnp.where(2 * mode < AZIM, mode, mode - AZIM)
        signed = jnp.where(2 * mode == AZIM, 0, signed).astype(F32)
        fields[0].append(pair[0])
        fields[1].append(pair[1])
        fields[2].append(pair[0] * signed)
    cosine = (table_ref[0:256, :], table_ref[512:768, :])
    sine = (table_ref[256:512, :], table_ref[768:1024, :])
    waves = []
    for field in range(3):
        left = _split(jnp.concatenate(fields[field], axis=0))
        waves.append((_dot3(left, cosine), _dot3(left, sine)))
    for a in range(8):
        tiles = []
        for field in range(3):
            total = None
            for n2 in range(8):
                even = waves[field][0][8 * n2 : 8 * n2 + 8, :]
                odd = waves[field][1][8 * n2 : 8 * n2 + 8, :]
                plus = twist_ref[8 * n2 + a : 8 * n2 + a + 1, :]
                minus = twist_ref[64 + 8 * n2 + a : 65 + 8 * n2 + a, :]
                if field < 2:
                    term = even * plus + odd * minus
                else:
                    term = even * minus - odd * plus
                total = term if total is None else total + term
            for zh in range(2):
                for half in range(2):
                    row = zh * 4 + half * 2
                    out_ref[a * 2 + zh, field * 2 + half] = total[row : row + 2, :]
            tiles.append(total)
        high, low = _split(jnp.concatenate(tiles, axis=0))
        both = jnp.concatenate([high, low], axis=0)
        for zh in range(2):
            cell = cells_ref[a * 2 + zh, 2]
            cell = jnp.concatenate([cell[0:1], cell[1:2]], axis=1).astype(jnp.int32)
            found = _dot(both, _one_hot(cell & 255, SECTOR))
            found = found[0:24] + found[24:48]
            weight = _dot(weight_ref[group, zh], _one_hot(lax.shift_right_logical(cell, 8), HEIGHTS))
            weight = weight[0:16] + weight[16:32]
            accel = [
                jnp.sum(weight[0:8] * found[8:16], axis=0, keepdims=True),
                jnp.sum(weight[0:8] * found[16:24], axis=0, keepdims=True),
                jnp.sum(weight[8:16] * found[0:8], axis=0, keepdims=True),
            ]
            for slot, dest in ((1, (a + 7) % 8), (0, (a + 1) % 8)):
                lanes = slice(0, CAP) if slot == 1 else slice(CAP, 2 * CAP)
                for field in range(3):
                    row = slot * 3 + field
                    out_ref[dest * 2 + zh, 6 + row // 2, row % 2 : row % 2 + 1, :] = accel[field][:, lanes]


def pick_kernel(positions_ref, velocities_ref, mass_ref, active_ref, lists_ref, counts_ref, wrap_ref, near_ref):
    wanted = jnp.concatenate([lists_ref[0:1, :], lists_ref[1:2, :]], axis=1)
    total = jnp.zeros((32, 2 * CAP), F32)
    for start in range(0, STARS, CHUNK):
        moving = jnp.concatenate(
            [positions_ref[:, start : start + CHUNK], velocities_ref[:, start : start + CHUNK]], axis=0
        )
        high = moving.astype(BF16).astype(F32)
        rest = moving - high
        middle = rest.astype(BF16).astype(F32)
        low = rest - middle
        plain = jnp.concatenate(
            [
                mass_ref[start : start + CHUNK].astype(F32).reshape(1, CHUNK),
                active_ref[:, start : start + CHUNK].astype(F32),
                jnp.zeros((6, CHUNK), F32),
            ],
            axis=0,
        )
        pad = jnp.zeros((2, CHUNK), F32)
        left = jnp.concatenate([high, pad, middle, pad, low, pad, plain], axis=0).astype(BF16)
        ids = lax.broadcasted_iota(jnp.int32, (CHUNK, 2 * CAP), 0) + start
        hot = jnp.where(ids == wanted, 1.0, 0.0).astype(BF16)
        total += _dot(left, hot)
    moving = (total[0:6] + total[8:14]) + total[16:22]
    slots = lax.broadcasted_iota(jnp.int32, (1, CAP), 1)
    keep = [jnp.where(slots < counts_ref[:, i : i + 1], 1.0, 0.0) for i in range(2)]
    rows = jnp.concatenate(
        [moving, total[24:26], jnp.concatenate(keep, axis=1), jnp.zeros((7, 2 * CAP), F32)], axis=0
    )
    down = rows[:, :CAP]
    up = rows[:, CAP:]
    odd = lax.rem(lax.axis_index("az"), 2) == 1
    wrap_ref[...] = jnp.where(odd, up, down)
    near_ref[...] = jnp.where(odd, down, up)


def _sample(fields, layer, angle):
    lanes = layer.shape[1]
    hot = _one_hot(angle, SECTOR)
    both = _dot(fields, hot)
    here = lax.broadcasted_iota(jnp.int32, (HEIGHTS, lanes), 0) == layer
    found = []
    for field in range(3):
        block = both[64 * field : 64 * field + 64] + both[192 + 64 * field : 256 + 64 * field]
        found.append(jnp.sum(jnp.where(here, block, 0.0), axis=0, keepdims=True))
    return found


def _advance(position, velocity, accel, live):
    radius = position[0]
    speed = [
        velocity[0] + live * accel[0],
        velocity[1] + live * (accel[1] / radius),
        velocity[2] + live * accel[2],
    ]
    place = [
        position[0] + live * speed[0],
        position[1] + live * (speed[1] / radius),
        position[2] + live * speed[2],
    ]
    return place + speed


def final_kernel(
    modes_ref, table_ref, far_ref, close_ref, positions_ref, velocities_ref, cells_ref, active_ref,
    grid_ref, state_ref, arrive_ref,
):
    pieces = [modes_ref[group, part] for group in range(16) for part in range(6)]
    modes = jnp.concatenate(pieces, axis=0)
    result = _dot3((table_ref[0:256, :], table_ref[256:512, :]), _split(modes))
    for h in range(HEIGHTS):
        grid_ref[h] = result[h : h + 1, :]
    field_high, field_low = _split(result[64:256])
    fields = jnp.concatenate([field_high, field_low], axis=0)

    sums = []
    for part in range(6, 9):
        total = modes_ref[0, part]
        for group in range(1, 16):
            total = total + modes_ref[group, part]
        sums += [total[0:1], total[1:2]]
    odd = lax.rem(lax.axis_index("az"), 2) == 1
    far = far_ref[...]
    close = close_ref[...]
    for slot in range(2):
        picked = jnp.where(odd, far, close) if slot else jnp.where(odd, close, far)
        state = _advance(
            [picked[i : i + 1] for i in range(3)],
            [picked[i : i + 1] for i in range(3, 6)],
            sums[slot * 3 : slot * 3 + 3],
            picked[7:8],
        )
        keep = picked[8:9] > 0.5
        for row, value in enumerate(state + [picked[6:7]]):
            arrive_ref[row, slot : slot + 1, :] = jnp.where(keep, value, 0.0)

    for start in range(0, STARS, CHUNK):
        lanes = slice(start, start + CHUNK)
        cell = cells_ref[:, lanes]
        accel = _sample(fields, lax.shift_right_logical(cell, 8), cell & 255)
        state = _advance(
            [positions_ref[i : i + 1, lanes] for i in range(3)],
            [velocities_ref[i : i + 1, lanes] for i in range(3)],
            accel,
            active_ref[:, lanes].astype(F32),
        )
        for row in range(6):
            state_ref[row : row + 1, lanes] = state[row]


def _call(kernel, out_shape, name, flops, in_smem=(), in_hbm=(), count=0, scratch=(), limit=48 << 20):
    vmem = pl.BlockSpec(memory_space=pltpu.VMEM)
    smem = pl.BlockSpec(memory_space=pltpu.SMEM)
    hbm = pl.BlockSpec(memory_space=pltpu.HBM)
    outs = jax.tree.map(lambda _: vmem, out_shape)
    return pl.pallas_call(
        kernel,
        out_shape=out_shape,
        in_specs=[smem if i in in_smem else hbm if i in in_hbm else vmem for i in range(count)],
        out_specs=outs,
        scratch_shapes=list(scratch),
        name=name,
        cost_estimate=pl.CostEstimate(flops=flops, bytes_accessed=1 << 20, transcendentals=0),
        compiler_params=pltpu.CompilerParams(vmem_limit_bytes=limit),
    )


def per_device(positions, velocities, masses, cells, active, send_lists, send_counts):
    shape = functools.partial(jax.ShapeDtypeStruct, dtype=F32)
    z_axes, plane_axes = ("az", "zh"), ("x", "y", "c")
    exchange = functools.partial(lax.all_to_all, split_axis=0, concat_axis=0, tiled=True)
    table = _split_np(_trig())
    twist = _twist()
    cell = cells.reshape(1, STARS)
    live = active.reshape(1, STARS)

    layered = _call(
        deposit_kernel,
        shape((16, 3, 2, SECTOR)),
        "deposit",
        10**9,
        in_hbm=(0, 1, 2),
        limit=None,
        count=3,
        scratch=[
            pltpu.VMEM((1, STARS), jnp.int32),
            pltpu.VMEM((STARS,), BF16),
            pltpu.VMEM((2, CAP), jnp.int32),
            pltpu.SemaphoreType.DMA((3,)),
        ],
    )(cell, masses, send_lists)
    layered, eigen, late_lists = lax.optimization_barrier((layered, jnp.asarray(_eigen()), send_lists))
    sectors = exchange(layered, z_axes)
    factors = _call(
        factor_kernel,
        (shape((64, SECTOR)), shape((64, SECTOR)), shape((64, SECTOR)), shape((8, SECTOR))),
        "factor",
        10**9,
        in_smem=(0,),
        count=1,
    )(eigen)
    wrap, near = _call(pick_kernel, (shape((16, CAP)), shape((16, CAP))), "pick", 10**9, count=6)(
        positions, velocities, masses, live, late_lists, send_counts.reshape(1, 2)
    )
    sectors, factors, wrap, near = lax.optimization_barrier((sectors, factors, wrap, near))
    spectrum = _call(forward_kernel, shape((32, 2, SECTOR)), "forward", 10**9, count=3)(
        sectors, twist, table
    )
    columns = exchange(spectrum, plane_axes)
    solved = _call(
        solve_kernel,
        shape((32, 4, SECTOR)),
        "solve",
        10**9,
        count=5,
        scratch=[pltpu.VMEM((64, SECTOR), F32)],
    )(columns, *factors)
    waves = exchange(solved, plane_axes)
    angles = _call(inverse_kernel, shape((16, 9, 2, SECTOR)), "inverse", 10**9, count=5)(
        waves, twist, table, sectors, _weight_table()
    )
    angles, wrap, near = lax.optimization_barrier((angles, wrap, near))
    modes = exchange(angles, z_axes)
    far = lax.ppermute(wrap, "az", [(i, (i + 1) % 8 if i % 2 else (i + 7) % 8) for i in range(8)])
    close = lax.ppermute(near, "az", [(i, i ^ 1) for i in range(8)])
    potential, state, arrivals = _call(
        final_kernel,
        (shape((64, 1, SECTOR)), shape((6, STARS)), shape((7, 2, CAP))),
        "final",
        10**9,
        count=8,
    )(modes, _split_np(_field_table()), far, close, positions, velocities, cell, live)
    return potential, state, arrivals.transpose(1, 0, 2)


def solution(mesh):
    fine = Mesh(mesh.devices.reshape(8, 4, 2, 4, 2), ("az", "x", "zh", "y", "c"))
    rz = ("x", "zh", "y", "c")
    every = ("az",) + rz
    return jax.shard_map(
        per_device,
        mesh=fine,
        in_specs=(
            P(None, every),
            P(None, every),
            P(every),
            P(every),
            P(every),
            P(None, every),
            P(None, every),
        ),
        out_specs=(P(None, rz, "az"), P(None, every), P(None, None, every)),
        check_vma=False,
    )
```

```python
import functools
import math

import jax
import jax.numpy as jnp
import numpy as np
from jax import lax
from jax.experimental import pallas as pl
from jax.experimental.pallas import tpu as pltpu
from jax.sharding import Mesh
from jax.sharding import PartitionSpec as P

HEIGHTS = 64
RADII = 64
AZIM = 2048
SECTOR = 256
STARS = 4096
CAP = 256
CHUNK = 512
INNER = 8.0

F32 = jnp.float32
BF16 = jnp.bfloat16


def _split_np(table):
    exact = np.asarray(table, np.float64)
    high = exact.astype(np.float32).astype(jnp.bfloat16)
    low = (exact - high.astype(np.float64)).astype(np.float32).astype(jnp.bfloat16)
    return np.concatenate([high, low], axis=0)


def _sine():
    levels = np.arange(HEIGHTS) + 1
    turns = levels[:, None] * levels[None, :] % (2 * (HEIGHTS + 1))
    return math.sqrt(2.0 / (HEIGHTS + 1)) * np.sin(turns * (math.pi / (HEIGHTS + 1)))


def _trig():
    ids = np.arange(SECTOR)
    theta = (ids[:, None] * ids[None, :] % SECTOR) * (2.0 * math.pi / SECTOR)
    return np.concatenate([np.cos(theta), np.sin(theta)], axis=0)


def _twist():
    residues = np.arange(8)
    angles = np.arange(AZIM)
    theta = (residues[:, None] * angles[None, :] % AZIM) * (2.0 * math.pi / AZIM)
    plus = np.cos(theta) + np.sin(theta)
    minus = np.cos(theta) - np.sin(theta)
    return np.concatenate([plus, minus], axis=0).reshape(128, SECTOR).astype(np.float32)


def _field_table():
    sine = _sine()
    shifted = np.zeros((HEIGHTS, HEIGHTS))
    shifted[:-1] += sine[1:]
    shifted[1:] -= sine[:-1]
    vertical = 0.5 * shifted
    table = np.zeros((4, HEIGHTS, 16, 3, 4))
    by_group = sine.reshape(HEIGHTS, 16, 4)
    table[0, :, :, 0, :] = by_group
    table[1, :, :, 1, :] = -by_group
    table[2, :, :, 2, :] = -by_group
    table[3, :, :, 0, :] = -vertical.reshape(HEIGHTS, 16, 4)
    return table.reshape(4 * HEIGHTS, 192) / AZIM


def _weight_table():
    table = _field_table().reshape(4, HEIGHTS, 16, 3, 4)
    exact = np.zeros((16, 2, 2, 4, 128), np.float32)
    exact[:, 0, :, :, :HEIGHTS] = table[1, :, :, 1, :].transpose(1, 2, 0)[:, None]
    exact[:, 1, :, :, :HEIGHTS] = table[3, :, :, 0, :].transpose(1, 2, 0)[:, None]
    return exact.reshape(16, 16, 128)


def _eigen():
    levels = np.arange(HEIGHTS) + 1.0
    return ((2.0 * np.sin(levels * (math.pi / (2 * (HEIGHTS + 1))))) ** 2).astype(np.float32)


def _row_of(radius):
    x, zh, y, c = radius >> 4, (radius >> 3) & 1, (radius >> 1) & 3, radius & 1
    return (((x * 4 + y) * 2 + c) * 2) + zh


def _split(value):
    high = value.astype(BF16)
    low = (value - high.astype(F32)).astype(BF16)
    return high, low


def _dot(a, b):
    return jnp.dot(a, b, preferred_element_type=F32)


def _dot3(a, b):
    (a_high, a_low), (b_high, b_low) = a, b
    return _dot(a_high, b_high) + (_dot(a_low, b_high) + _dot(a_high, b_low))


def _rows(rows, lanes):
    return lax.broadcasted_iota(jnp.int32, (rows, lanes), 0).astype(F32).astype(BF16)


def _one_hot(ids, rows):
    lanes = ids.shape[1]
    small = jnp.broadcast_to(ids.astype(F32).astype(BF16), (rows, lanes))
    here = _rows(rows, lanes) == small
    return jnp.where(here, jnp.ones((), BF16), jnp.zeros((), BF16))


def _star_hot(wanted, start):
    offset = wanted - start
    inside = (offset >= 0) & (offset < 256)
    return _one_hot(jnp.where(inside, offset, -1), 256)


def _sine_in_kernel():
    shape = (HEIGHTS, HEIGHTS)
    first = lax.broadcasted_iota(jnp.int32, shape, 0) + 1
    second = lax.broadcasted_iota(jnp.int32, shape, 1) + 1
    turns = lax.rem(first * second, 2 * (HEIGHTS + 1))
    negative = turns > HEIGHTS + 1
    turns = jnp.where(negative, turns - (HEIGHTS + 1), turns)
    turns = jnp.minimum(turns, HEIGHTS + 1 - turns).astype(F32)
    angle = turns * (math.pi / (HEIGHTS + 1))
    square = angle * angle
    series = jnp.full(shape, 1.0 / math.factorial(13), F32)
    for power in (11, 9, 7, 5, 3, 1):
        sign = -1.0 if power % 4 == 3 else 1.0
        series = series * square + sign / math.factorial(power)
    value = series * angle * math.sqrt(2.0 / (HEIGHTS + 1))
    return jnp.where(negative, -value, value)


def _lanes_of(table, ids):
    return jnp.take_along_axis(table, ids, axis=1)


def deposit_kernel(cells_hbm, mass_hbm, lists_hbm, square_hbm, out_ref, cells_ref, mass_ref, lists_ref, square_ref, sems):
    cells_copy = pltpu.make_async_copy(cells_hbm, cells_ref, sems.at[0])
    mass_copy = pltpu.make_async_copy(mass_hbm, mass_ref, sems.at[1])
    lists_copy = pltpu.make_async_copy(lists_hbm, lists_ref, sems.at[2])
    cells_copy.start()
    square_copy = pltpu.make_async_copy(square_hbm, square_ref, sems.at[3])
    lists_copy.start()
    mass_copy.start()
    square_copy.start()
    sine = _split(_sine_in_kernel())
    cells_copy.wait()
    lists_copy.wait()
    mass_copy.wait()
    square_copy.wait()
    wanted = [lists_ref[i : i + 1, half : half + 128] for i in range(2) for half in (0, 128)]
    wanted = jnp.concatenate(wanted + wanted, axis=0)
    lane = wanted & 127
    line = lax.shift_right_logical(wanted, 7)
    sent = jnp.zeros((8, 128), jnp.int32)
    for row in range(STARS // 128):
        found = _lanes_of(jnp.broadcast_to(square_ref[row : row + 1, :], (8, 128)), lane)
        sent = jnp.where(line == row, found, sent)
    sent = sent.astype(F32)
    total = jnp.zeros((HEIGHTS, SECTOR), F32)
    for start in range(0, STARS, CHUNK):
        cell = cells_ref[:, start : start + CHUNK]
        mass = mass_ref[start : start + CHUNK].astype(F32).reshape(1, CHUNK)
        layer = lax.shift_right_logical(cell, 8)
        angle = cell & 255
        here = lax.broadcasted_iota(jnp.int32, (HEIGHTS, CHUNK), 0) == layer
        left = jnp.where(here, mass, 0.0).astype(BF16)
        right = _one_hot(angle, SECTOR)
        total += lax.dot_general(
            left, right, (((1,), (1,)), ((), ())), preferred_element_type=F32
        )
    layered = _dot3(sine, _split(total))
    cells_sent = [jnp.concatenate([sent[2 * i : 2 * i + 1], sent[2 * i + 1 : 2 * i + 2]], axis=1) for i in range(2)]
    for group in range(16):
        out_ref[group, 0] = layered[4 * group : 4 * group + 2, :]
        out_ref[group, 1] = layered[4 * group + 2 : 4 * group + 4, :]
        out_ref[group, 2, 0:1, :] = cells_sent[0]
        out_ref[group, 2, 1:2, :] = cells_sent[1]


def forward_kernel(x_ref, twist_ref, table_ref, out_ref):
    tiles = []
    for a in range(8):
        parts = [x_ref[2 * a + zh, half] for zh in range(2) for half in range(2)]
        tiles.append(jnp.concatenate(parts, axis=0))
    rows = []
    for n2 in range(8):
        even = None
        odd = None
        for a in range(8):
            at = 8 * n2 + a
            plus = tiles[a] * twist_ref[at : at + 1, :]
            minus = tiles[a] * twist_ref[64 + at : 65 + at, :]
            even = plus if even is None else even + plus
            odd = minus if odd is None else odd + minus
        rows.append(jnp.concatenate([even, odd], axis=1))
    left = _split(jnp.concatenate(rows, axis=0))
    result = _dot3(left, (table_ref[0:512, :], table_ref[512:1024, :]))
    for n2 in range(8):
        for k in range(4):
            for zh in range(2):
                at = n2 * 8 + zh * 4 + k
                out_ref[n2 * 4 + k, zh : zh + 1, :] = result[at : at + 1, :]


def factor_kernel(eigen_ref, inverse_ref, carry_ref, factor_ref, joint_ref):
    group = lax.axis_index("az") * 2 + lax.axis_index("zh")
    place = (lax.axis_index("x") * 4 + lax.axis_index("y")) * 2 + lax.axis_index("c")
    level = group * 4 + lax.rem(place, 4)
    residue = lax.div(place, 4)
    eigen = eigen_ref[level]
    mode = lax.broadcasted_iota(jnp.int32, (1, SECTOR), 1) * 8 + residue
    mode = jnp.minimum(mode, AZIM - mode).astype(F32)
    square = mode * mode
    top = None
    bottom = None
    for step in range(RADII // 2):
        i = step
        radius = INNER + i + 0.5
        lower = -(radius - 0.5) / radius
        upper = -(radius + 0.5) / radius
        denom = (2.0 + eigen) + square * (1.0 / (radius * radius))
        if top is not None:
            denom = denom - lower * top
        inverse = 1.0 / denom
        top = upper * inverse
        row = _row_of(i)
        inverse_ref[row : row + 1, :] = -inverse
        carry_ref[row : row + 1, :] = -lower * inverse
        factor_ref[row : row + 1, :] = -top
        i = RADII - 1 - step
        radius = INNER + i + 0.5
        lower = -(radius - 0.5) / radius
        upper = -(radius + 0.5) / radius
        denom = (2.0 + eigen) + square * (1.0 / (radius * radius))
        if bottom is not None:
            denom = denom - upper * bottom
        inverse = 1.0 / denom
        bottom = lower * inverse
        row = _row_of(i)
        inverse_ref[row : row + 1, :] = -inverse
        carry_ref[row : row + 1, :] = -upper * inverse
        factor_ref[row : row + 1, :] = -bottom
    joint_ref[...] = jnp.broadcast_to(1.0 / (1.0 - top * bottom), (8, SECTOR))


def solve_kernel(source_ref, inverse_ref, carry_ref, factor_ref, joint_ref, out_ref, scaled_ref):
    half = RADII // 2
    for place in range(32):
        rows = slice(2 * place, 2 * place + 2)
        scaled_ref[rows, :] = source_ref[place] * inverse_ref[rows, :]

    def at(ref, i):
        row = _row_of(i)
        return ref[row : row + 1, :]

    values = [None] * RADII
    values[0] = at(scaled_ref, 0)
    values[RADII - 1] = at(scaled_ref, RADII - 1)
    for step in range(1, half):
        i = step
        values[i] = at(scaled_ref, i) + at(carry_ref, i) * values[i - 1]
        i = RADII - 1 - step
        values[i] = at(scaled_ref, i) + at(carry_ref, i) * values[i + 1]
    solved = [None] * RADII
    solved[half - 1] = (values[half - 1] + at(factor_ref, half - 1) * values[half]) * joint_ref[0:1, :]
    solved[half] = values[half] + at(factor_ref, half) * solved[half - 1]
    for step in range(1, half):
        i = half - 1 - step
        solved[i] = values[i] + at(factor_ref, i) * solved[i + 1]
        i = half + step
        solved[i] = values[i] + at(factor_ref, i) * solved[i - 1]
    for i in range(RADII):
        row = _row_of(i)
        place, zh = row >> 1, row & 1
        out_ref[place, zh : zh + 1, :] = solved[i]
        if i == 0:
            slope = solved[1] * 0.5
        elif i == RADII - 1:
            slope = solved[RADII - 2] * -0.5
        else:
            slope = (solved[i + 1] - solved[i - 1]) * 0.5
        out_ref[place, zh + 2 : zh + 3, :] = slope


def inverse_kernel(x_ref, twist_ref, table_ref, cells_ref, weight_ref, out_ref):
    group = lax.axis_index("az") * 2 + lax.axis_index("zh")
    fields = [[], [], []]
    for n2 in range(8):
        pair = []
        for field in range(2):
            spots = [(n2 * 4 + k, field * 2 + zh) for zh in range(2) for k in range(4)]
            pair.append(jnp.concatenate([x_ref[at, row : row + 1, :] for at, row in spots], axis=0))
        mode = lax.broadcasted_iota(jnp.int32, (8, SECTOR), 1) * 8 + n2
        signed = jnp.where(2 * mode < AZIM, mode, mode - AZIM)
        signed = jnp.where(2 * mode == AZIM, 0, signed).astype(F32)
        fields[0].append(pair[0])
        fields[1].append(pair[1])
        fields[2].append(pair[0] * signed)
    cosine = (table_ref[0:256, :], table_ref[512:768, :])
    sine = (table_ref[256:512, :], table_ref[768:1024, :])
    waves = []
    for field in range(3):
        left = _split(jnp.concatenate(fields[field], axis=0))
        waves.append((_dot3(left, cosine), _dot3(left, sine)))
    for a in range(8):
        tiles = []
        for field in range(3):
            total = None
            for n2 in range(8):
                even = waves[field][0][8 * n2 : 8 * n2 + 8, :]
                odd = waves[field][1][8 * n2 : 8 * n2 + 8, :]
                plus = twist_ref[8 * n2 + a : 8 * n2 + a + 1, :]
                minus = twist_ref[64 + 8 * n2 + a : 65 + 8 * n2 + a, :]
                if field < 2:
                    term = even * plus + odd * minus
                else:
                    term = even * minus - odd * plus
                total = term if total is None else total + term
            for zh in range(2):
                for half in range(2):
                    row = zh * 4 + half * 2
                    out_ref[a * 2 + zh, field * 2 + half] = total[row : row + 2, :]
            tiles.append(total)
        accel = [[], [], []]
        for quarter in range(4):
            at = 128 * (quarter % 2)
            cell = [cells_ref[a * 2 + zh, 2, quarter // 2 : quarter // 2 + 1, at : at + 128] for zh in range(2)]
            cell = jnp.concatenate([jnp.broadcast_to(part, (4, 128)) for part in cell], axis=0).astype(jnp.int32)
            layer = lax.shift_right_logical(cell, 8)
            lane = cell & 127
            upper = (cell & 128) == 128
            found = [
                jnp.where(upper, _lanes_of(tile[:, 128:], lane), _lanes_of(tile[:, :128], lane))
                for tile in tiles
            ]
            sine_at = _lanes_of(weight_ref[group, 0:8, :], layer)
            step_at = _lanes_of(weight_ref[group, 8:16, :], layer)
            for field, term in enumerate((sine_at * found[1], sine_at * found[2], step_at * found[0])):
                term = term + pltpu.roll(term, 2, axis=0)
                accel[field].append(term + pltpu.roll(term, 1, axis=0))
        for field in range(3):
            for slot, dest, first in ((1, (a + 7) % 8, 0), (0, (a + 1) % 8, 2)):
                pair = jnp.concatenate(accel[field][first : first + 2], axis=1)
                row = slot * 3 + field
                for zh in range(2):
                    spot = 4 * zh + 3
                    out_ref[dest * 2 + zh, 6 + row // 2, row % 2 : row % 2 + 1, :] = pair[spot : spot + 1, :]


def pick_kernel(positions_ref, velocities_ref, mass_ref, active_ref, lists_ref, counts_ref, wrap_ref, near_ref):
    wanted = jnp.concatenate([lists_ref[0:1, :], lists_ref[1:2, :]], axis=1)
    total = jnp.zeros((32, 2 * CAP), F32)
    for start in range(0, STARS, CHUNK):
        moving = jnp.concatenate(
            [positions_ref[:, start : start + CHUNK], velocities_ref[:, start : start + CHUNK]], axis=0
        )
        high = moving.astype(BF16).astype(F32)
        rest = moving - high
        middle = rest.astype(BF16).astype(F32)
        low = rest - middle
        plain = jnp.concatenate(
            [
                mass_ref[start : start + CHUNK].astype(F32).reshape(1, CHUNK),
                active_ref[:, start : start + CHUNK].astype(F32),
                jnp.zeros((6, CHUNK), F32),
            ],
            axis=0,
        )
        pad = jnp.zeros((2, CHUNK), F32)
        left = jnp.concatenate([high, pad, middle, pad, low, pad, plain], axis=0).astype(BF16)
        hot = jnp.concatenate([_star_hot(wanted, start), _star_hot(wanted, start + 256)], axis=0)
        total += _dot(left, hot)
    moving = (total[0:6] + total[8:14]) + total[16:22]
    slots = lax.broadcasted_iota(jnp.int32, (1, CAP), 1)
    keep = [jnp.where(slots < counts_ref[:, i : i + 1], 1.0, 0.0) for i in range(2)]
    rows = jnp.concatenate(
        [moving, total[24:26], jnp.concatenate(keep, axis=1), jnp.zeros((7, 2 * CAP), F32)], axis=0
    )
    down = rows[:, :CAP]
    up = rows[:, CAP:]
    odd = lax.rem(lax.axis_index("az"), 2) == 1
    wrap_ref[...] = jnp.where(odd, up, down)
    near_ref[...] = jnp.where(odd, down, up)


def _sample(fields, layer, angle):
    lanes = layer.shape[1]
    hot = _one_hot(angle, SECTOR)
    both = _dot(fields, hot)
    here = lax.broadcasted_iota(jnp.int32, (HEIGHTS, lanes), 0) == layer
    found = []
    for field in range(3):
        block = both[64 * field : 64 * field + 64] + both[192 + 64 * field : 256 + 64 * field]
        found.append(jnp.sum(jnp.where(here, block, 0.0), axis=0, keepdims=True))
    return found


def _advance(position, velocity, accel, live):
    radius = position[0]
    speed = [
        velocity[0] + live * accel[0],
        velocity[1] + live * (accel[1] / radius),
        velocity[2] + live * accel[2],
    ]
    place = [
        position[0] + live * speed[0],
        position[1] + live * (speed[1] / radius),
        position[2] + live * speed[2],
    ]
    return place + speed


def final_kernel(
    modes_ref, table_ref, far_ref, close_ref, positions_ref, velocities_ref, cells_ref, active_ref,
    grid_ref, state_ref, arrive_ref,
):
    pieces = [modes_ref[group, part] for group in range(16) for part in range(6)]
    modes = jnp.concatenate(pieces, axis=0)
    result = _dot3((table_ref[0:256, :], table_ref[256:512, :]), _split(modes))
    for h in range(HEIGHTS):
        grid_ref[h] = result[h : h + 1, :]
    field_high, field_low = _split(result[64:256])
    fields = jnp.concatenate([field_high, field_low], axis=0)

    sums = []
    for part in range(6, 9):
        total = modes_ref[0, part]
        for group in range(1, 16):
            total = total + modes_ref[group, part]
        sums += [total[0:1], total[1:2]]
    odd = lax.rem(lax.axis_index("az"), 2) == 1
    far = far_ref[...]
    close = close_ref[...]
    for slot in range(2):
        picked = jnp.where(odd, far, close) if slot else jnp.where(odd, close, far)
        state = _advance(
            [picked[i : i + 1] for i in range(3)],
            [picked[i : i + 1] for i in range(3, 6)],
            sums[slot * 3 : slot * 3 + 3],
            picked[7:8],
        )
        keep = picked[8:9] > 0.5
        for row, value in enumerate(state + [picked[6:7]]):
            arrive_ref[row, slot : slot + 1, :] = jnp.where(keep, value, 0.0)

    for start in range(0, STARS, CHUNK):
        lanes = slice(start, start + CHUNK)
        cell = cells_ref[:, lanes]
        accel = _sample(fields, lax.shift_right_logical(cell, 8), cell & 255)
        state = _advance(
            [positions_ref[i : i + 1, lanes] for i in range(3)],
            [velocities_ref[i : i + 1, lanes] for i in range(3)],
            accel,
            active_ref[:, lanes].astype(F32),
        )
        for row in range(6):
            state_ref[row : row + 1, lanes] = state[row]


def _call(kernel, out_shape, name, flops, in_smem=(), in_hbm=(), count=0, scratch=(), limit=48 << 20):
    vmem = pl.BlockSpec(memory_space=pltpu.VMEM)
    smem = pl.BlockSpec(memory_space=pltpu.SMEM)
    hbm = pl.BlockSpec(memory_space=pltpu.HBM)
    outs = jax.tree.map(lambda _: vmem, out_shape)
    return pl.pallas_call(
        kernel,
        out_shape=out_shape,
        in_specs=[smem if i in in_smem else hbm if i in in_hbm else vmem for i in range(count)],
        out_specs=outs,
        scratch_shapes=list(scratch),
        name=name,
        cost_estimate=pl.CostEstimate(flops=flops, bytes_accessed=1 << 20, transcendentals=0),
        compiler_params=pltpu.CompilerParams(vmem_limit_bytes=limit),
    )


def per_device(positions, velocities, masses, cells, active, send_lists, send_counts):
    shape = functools.partial(jax.ShapeDtypeStruct, dtype=F32)
    z_axes, plane_axes = ("az", "zh"), ("x", "y", "c")
    exchange = functools.partial(lax.all_to_all, split_axis=0, concat_axis=0, tiled=True)
    table = _split_np(_trig())
    twist = _twist()
    cell = cells.reshape(1, STARS)
    live = active.reshape(1, STARS)

    layered = _call(
        deposit_kernel,
        shape((16, 3, 2, SECTOR)),
        "deposit",
        10**9,
        in_hbm=(0, 1, 2, 3),
        limit=None,
        count=4,
        scratch=[
            pltpu.VMEM((1, STARS), jnp.int32),
            pltpu.VMEM((STARS,), BF16),
            pltpu.VMEM((2, CAP), jnp.int32),
            pltpu.VMEM((STARS // 128, 128), jnp.int32),
            pltpu.SemaphoreType.DMA((4,)),
        ],
    )(cell, masses, send_lists, cells.reshape(STARS // 128, 128))
    layered, eigen, late_lists = lax.optimization_barrier((layered, jnp.asarray(_eigen()), send_lists))
    sectors = exchange(layered, z_axes)
    factors = _call(
        factor_kernel,
        (shape((64, SECTOR)), shape((64, SECTOR)), shape((64, SECTOR)), shape((8, SECTOR))),
        "factor",
        10**9,
        in_smem=(0,),
        count=1,
    )(eigen)
    wrap, near = _call(pick_kernel, (shape((16, CAP)), shape((16, CAP))), "pick", 10**9, count=6)(
        positions, velocities, masses, live, late_lists, send_counts.reshape(1, 2)
    )
    sectors, factors, wrap, near = lax.optimization_barrier((sectors, factors, wrap, near))
    spectrum = _call(forward_kernel, shape((32, 2, SECTOR)), "forward", 10**9, count=3)(
        sectors, twist, table
    )
    columns = exchange(spectrum, plane_axes)
    solved = _call(
        solve_kernel,
        shape((32, 4, SECTOR)),
        "solve",
        10**9,
        count=5,
        scratch=[pltpu.VMEM((64, SECTOR), F32)],
    )(columns, *factors)
    waves = exchange(solved, plane_axes)
    angles = _call(inverse_kernel, shape((16, 9, 2, SECTOR)), "inverse", 10**9, count=5)(
        waves, twist, table, sectors, _weight_table()
    )
    angles, wrap, near = lax.optimization_barrier((angles, wrap, near))
    modes = exchange(angles, z_axes)
    far = lax.ppermute(wrap, "az", [(i, (i + 1) % 8 if i % 2 else (i + 7) % 8) for i in range(8)])
    close = lax.ppermute(near, "az", [(i, i ^ 1) for i in range(8)])
    potential, state, arrivals = _call(
        final_kernel,
        (shape((64, 1, SECTOR)), shape((6, STARS)), shape((7, 2, CAP))),
        "final",
        10**9,
        count=8,
    )(modes, _split_np(_field_table()), far, close, positions, velocities, cell, live)
    return potential, state, arrivals.transpose(1, 0, 2)


def solution(mesh):
    fine = Mesh(mesh.devices.reshape(8, 4, 2, 4, 2), ("az", "x", "zh", "y", "c"))
    rz = ("x", "zh", "y", "c")
    every = ("az",) + rz
    return jax.shard_map(
        per_device,
        mesh=fine,
        in_specs=(
            P(None, every),
            P(None, every),
            P(every),
            P(every),
            P(every),
            P(None, every),
            P(None, every),
        ),
        out_specs=(P(None, rz, "az"), P(None, every), P(None, None, every)),
        check_vma=False,
    )
```

```python
import functools
import math

import jax
import jax.numpy as jnp
import numpy as np
from jax import lax
from jax.experimental import pallas as pl
from jax.experimental.pallas import tpu as pltpu
from jax.sharding import Mesh
from jax.sharding import PartitionSpec as P

HEIGHTS = 64
RADII = 64
AZIM = 2048
SECTOR = 256
STARS = 4096
CAP = 256
CHUNK = 512
INNER = 8.0

F32 = jnp.float32
BF16 = jnp.bfloat16


def _split_np(table):
    exact = np.asarray(table, np.float64)
    high = exact.astype(np.float32).astype(jnp.bfloat16)
    low = (exact - high.astype(np.float64)).astype(np.float32).astype(jnp.bfloat16)
    return np.concatenate([high, low], axis=0)


def _sine():
    levels = np.arange(HEIGHTS) + 1
    turns = levels[:, None] * levels[None, :] % (2 * (HEIGHTS + 1))
    return math.sqrt(2.0 / (HEIGHTS + 1)) * np.sin(turns * (math.pi / (HEIGHTS + 1)))


def _trig():
    ids = np.arange(SECTOR)
    theta = (ids[:, None] * ids[None, :] % SECTOR) * (2.0 * math.pi / SECTOR)
    return np.concatenate([np.cos(theta), np.sin(theta)], axis=0)


def _twist():
    residues = np.arange(8)
    angles = np.arange(AZIM)
    theta = (residues[:, None] * angles[None, :] % AZIM) * (2.0 * math.pi / AZIM)
    plus = np.cos(theta) + np.sin(theta)
    minus = np.cos(theta) - np.sin(theta)
    return np.concatenate([plus, minus], axis=0).reshape(128, SECTOR).astype(np.float32)


def _field_table():
    sine = _sine()
    shifted = np.zeros((HEIGHTS, HEIGHTS))
    shifted[:-1] += sine[1:]
    shifted[1:] -= sine[:-1]
    vertical = 0.5 * shifted
    table = np.zeros((4, HEIGHTS, 16, 3, 4))
    by_group = sine.reshape(HEIGHTS, 16, 4)
    table[0, :, :, 0, :] = by_group
    table[1, :, :, 1, :] = -by_group
    table[2, :, :, 2, :] = -by_group
    table[3, :, :, 0, :] = -vertical.reshape(HEIGHTS, 16, 4)
    return table.reshape(4 * HEIGHTS, 192) / AZIM


def _weight_table():
    table = _field_table().reshape(4, HEIGHTS, 16, 3, 4)
    exact = np.zeros((16, 2, 2, 4, 128), np.float32)
    exact[:, 0, :, :, :HEIGHTS] = table[1, :, :, 1, :].transpose(1, 2, 0)[:, None]
    exact[:, 1, :, :, :HEIGHTS] = table[3, :, :, 0, :].transpose(1, 2, 0)[:, None]
    return exact.reshape(16, 16, 128)


def _eigen():
    levels = np.arange(HEIGHTS) + 1.0
    return ((2.0 * np.sin(levels * (math.pi / (2 * (HEIGHTS + 1))))) ** 2).astype(np.float32)


def _row_of(radius):
    x, zh, y, c = radius >> 4, (radius >> 3) & 1, (radius >> 1) & 3, radius & 1
    return (((y * 2 + c) * 4 + x) * 2) + zh


def _split(value):
    high = value.astype(BF16)
    low = (value - high.astype(F32)).astype(BF16)
    return high, low


def _dot(a, b):
    return jnp.dot(a, b, preferred_element_type=F32)


def _dot3(a, b):
    (a_high, a_low), (b_high, b_low) = a, b
    return _dot(a_high, b_high) + (_dot(a_low, b_high) + _dot(a_high, b_low))


def _rows(rows, lanes):
    return lax.broadcasted_iota(jnp.int32, (rows, lanes), 0).astype(F32).astype(BF16)


def _one_hot(ids, rows):
    lanes = ids.shape[1]
    small = jnp.broadcast_to(ids.astype(F32).astype(BF16), (rows, lanes))
    here = _rows(rows, lanes) == small
    return jnp.where(here, jnp.ones((), BF16), jnp.zeros((), BF16))


def _star_hot(wanted, start):
    offset = wanted - start
    inside = (offset >= 0) & (offset < 256)
    return _one_hot(jnp.where(inside, offset, -1), 256)


def _sine_in_kernel():
    shape = (HEIGHTS, HEIGHTS)
    first = lax.broadcasted_iota(jnp.int32, shape, 0) + 1
    second = lax.broadcasted_iota(jnp.int32, shape, 1) + 1
    turns = lax.rem(first * second, 2 * (HEIGHTS + 1))
    negative = turns > HEIGHTS + 1
    turns = jnp.where(negative, turns - (HEIGHTS + 1), turns)
    turns = jnp.minimum(turns, HEIGHTS + 1 - turns).astype(F32)
    angle = turns * (math.pi / (HEIGHTS + 1))
    square = angle * angle
    series = jnp.full(shape, 1.0 / math.factorial(13), F32)
    for power in (11, 9, 7, 5, 3, 1):
        sign = -1.0 if power % 4 == 3 else 1.0
        series = series * square + sign / math.factorial(power)
    value = series * angle * math.sqrt(2.0 / (HEIGHTS + 1))
    return jnp.where(negative, -value, value)


def _lanes_of(table, ids):
    return jnp.take_along_axis(table, ids, axis=1)


def deposit_kernel(cells_hbm, mass_hbm, lists_hbm, square_hbm, out_ref, cells_ref, mass_ref, lists_ref, square_ref, sems):
    cells_copy = pltpu.make_async_copy(cells_hbm, cells_ref, sems.at[0])
    mass_copy = pltpu.make_async_copy(mass_hbm, mass_ref, sems.at[1])
    lists_copy = pltpu.make_async_copy(lists_hbm, lists_ref, sems.at[2])
    cells_copy.start()
    square_copy = pltpu.make_async_copy(square_hbm, square_ref, sems.at[3])
    lists_copy.start()
    mass_copy.start()
    square_copy.start()
    sine = _split(_sine_in_kernel())
    cells_copy.wait()
    lists_copy.wait()
    mass_copy.wait()
    square_copy.wait()
    wanted = [lists_ref[i : i + 1, half : half + 128] for i in range(2) for half in (0, 128)]
    wanted = jnp.concatenate(wanted + wanted, axis=0)
    lane = wanted & 127
    line = lax.shift_right_logical(wanted, 7)
    sent = jnp.zeros((8, 128), jnp.int32)
    for row in range(STARS // 128):
        found = _lanes_of(jnp.broadcast_to(square_ref[row : row + 1, :], (8, 128)), lane)
        sent = jnp.where(line == row, found, sent)
    sent = sent.astype(F32)
    total = jnp.zeros((HEIGHTS, SECTOR), F32)
    for start in range(0, STARS, CHUNK):
        cell = cells_ref[:, start : start + CHUNK]
        mass = mass_ref[start : start + CHUNK].astype(F32).reshape(1, CHUNK)
        layer = lax.shift_right_logical(cell, 8)
        angle = cell & 255
        here = lax.broadcasted_iota(jnp.int32, (HEIGHTS, CHUNK), 0) == layer
        left = jnp.where(here, mass, 0.0).astype(BF16)
        right = _one_hot(angle, SECTOR)
        total += lax.dot_general(
            left, right, (((1,), (1,)), ((), ())), preferred_element_type=F32
        )
    layered = _dot3(sine, _split(total))
    cells_sent = [jnp.concatenate([sent[2 * i : 2 * i + 1], sent[2 * i + 1 : 2 * i + 2]], axis=1) for i in range(2)]
    for group in range(16):
        out_ref[group, 0] = layered[4 * group : 4 * group + 2, :]
        out_ref[group, 1] = layered[4 * group + 2 : 4 * group + 4, :]
        out_ref[group, 2, 0:1, :] = cells_sent[0]
        out_ref[group, 2, 1:2, :] = cells_sent[1]


def forward_kernel(x_ref, twist_ref, table_ref, out_ref):
    tiles = []
    for a in range(8):
        parts = [x_ref[zh * 8 + a, half] for zh in range(2) for half in range(2)]
        tiles.append(jnp.concatenate(parts, axis=0))
    rows = []
    for n2 in range(8):
        even = None
        odd = None
        for a in range(8):
            at = 8 * n2 + a
            plus = tiles[a] * twist_ref[at : at + 1, :]
            minus = tiles[a] * twist_ref[64 + at : 65 + at, :]
            even = plus if even is None else even + plus
            odd = minus if odd is None else odd + minus
        rows.append(jnp.concatenate([even, odd], axis=1))
    left = _split(jnp.concatenate(rows, axis=0))
    result = _dot3(left, (table_ref[0:512, :], table_ref[512:1024, :]))
    for n2 in range(8):
        for k in range(4):
            for zh in range(2):
                at = n2 * 8 + zh * 4 + k
                out_ref[n2 * 4 + k, zh : zh + 1, :] = result[at : at + 1, :]


def factor_kernel(eigen_ref, inverse_ref, carry_ref, factor_ref, joint_ref):
    group = lax.axis_index("zh") * 8 + lax.axis_index("az")
    place = (lax.axis_index("y") * 2 + lax.axis_index("c")) * 4 + lax.axis_index("x")
    level = group * 4 + lax.rem(place, 4)
    residue = lax.div(place, 4)
    eigen = eigen_ref[level]
    mode = lax.broadcasted_iota(jnp.int32, (1, SECTOR), 1) * 8 + residue
    mode = jnp.minimum(mode, AZIM - mode).astype(F32)
    square = mode * mode
    top = None
    bottom = None
    for step in range(RADII // 2):
        i = step
        radius = INNER + i + 0.5
        lower = -(radius - 0.5) / radius
        upper = -(radius + 0.5) / radius
        denom = (2.0 + eigen) + square * (1.0 / (radius * radius))
        if top is not None:
            denom = denom - lower * top
        inverse = 1.0 / denom
        top = upper * inverse
        row = _row_of(i)
        inverse_ref[row : row + 1, :] = -inverse
        carry_ref[row : row + 1, :] = -lower * inverse
        factor_ref[row : row + 1, :] = -top
        i = RADII - 1 - step
        radius = INNER + i + 0.5
        lower = -(radius - 0.5) / radius
        upper = -(radius + 0.5) / radius
        denom = (2.0 + eigen) + square * (1.0 / (radius * radius))
        if bottom is not None:
            denom = denom - upper * bottom
        inverse = 1.0 / denom
        bottom = lower * inverse
        row = _row_of(i)
        inverse_ref[row : row + 1, :] = -inverse
        carry_ref[row : row + 1, :] = -upper * inverse
        factor_ref[row : row + 1, :] = -bottom
    joint_ref[...] = jnp.broadcast_to(1.0 / (1.0 - top * bottom), (8, SECTOR))


def solve_kernel(source_ref, inverse_ref, carry_ref, factor_ref, joint_ref, out_ref, scaled_ref):
    half = RADII // 2
    for place in range(32):
        rows = slice(2 * place, 2 * place + 2)
        scaled_ref[rows, :] = source_ref[place] * inverse_ref[rows, :]

    def at(ref, i):
        row = _row_of(i)
        return ref[row : row + 1, :]

    values = [None] * RADII
    values[0] = at(scaled_ref, 0)
    values[RADII - 1] = at(scaled_ref, RADII - 1)
    for step in range(1, half):
        i = step
        values[i] = at(scaled_ref, i) + at(carry_ref, i) * values[i - 1]
        i = RADII - 1 - step
        values[i] = at(scaled_ref, i) + at(carry_ref, i) * values[i + 1]
    solved = [None] * RADII
    solved[half - 1] = (values[half - 1] + at(factor_ref, half - 1) * values[half]) * joint_ref[0:1, :]
    solved[half] = values[half] + at(factor_ref, half) * solved[half - 1]
    for step in range(1, half):
        i = half - 1 - step
        solved[i] = values[i] + at(factor_ref, i) * solved[i + 1]
        i = half + step
        solved[i] = values[i] + at(factor_ref, i) * solved[i - 1]
    for i in range(RADII):
        row = _row_of(i)
        place, zh = row >> 1, row & 1
        out_ref[place, zh : zh + 1, :] = solved[i]
        if i == 0:
            slope = solved[1] * 0.5
        elif i == RADII - 1:
            slope = solved[RADII - 2] * -0.5
        else:
            slope = (solved[i + 1] - solved[i - 1]) * 0.5
        out_ref[place, zh + 2 : zh + 3, :] = slope


def inverse_kernel(x_ref, twist_ref, table_ref, cells_ref, weight_ref, out_ref):
    group = lax.axis_index("zh") * 8 + lax.axis_index("az")
    fields = [[], [], []]
    for n2 in range(8):
        pair = []
        for field in range(2):
            spots = [(n2 * 4 + k, field * 2 + zh) for zh in range(2) for k in range(4)]
            pair.append(jnp.concatenate([x_ref[at, row : row + 1, :] for at, row in spots], axis=0))
        mode = lax.broadcasted_iota(jnp.int32, (8, SECTOR), 1) * 8 + n2
        signed = jnp.where(2 * mode < AZIM, mode, mode - AZIM)
        signed = jnp.where(2 * mode == AZIM, 0, signed).astype(F32)
        fields[0].append(pair[0])
        fields[1].append(pair[1])
        fields[2].append(pair[0] * signed)
    cosine = (table_ref[0:256, :], table_ref[512:768, :])
    sine = (table_ref[256:512, :], table_ref[768:1024, :])
    waves = []
    for field in range(3):
        left = _split(jnp.concatenate(fields[field], axis=0))
        waves.append((_dot3(left, cosine), _dot3(left, sine)))
    for a in range(8):
        tiles = []
        for field in range(3):
            total = None
            for n2 in range(8):
                even = waves[field][0][8 * n2 : 8 * n2 + 8, :]
                odd = waves[field][1][8 * n2 : 8 * n2 + 8, :]
                plus = twist_ref[8 * n2 + a : 8 * n2 + a + 1, :]
                minus = twist_ref[64 + 8 * n2 + a : 65 + 8 * n2 + a, :]
                if field < 2:
                    term = even * plus + odd * minus
                else:
                    term = even * minus - odd * plus
                total = term if total is None else total + term
            for zh in range(2):
                for half in range(2):
                    row = zh * 4 + half * 2
                    out_ref[zh * 8 + a, field * 2 + half] = total[row : row + 2, :]
            tiles.append(total)
        accel = [[], [], []]
        for quarter in range(4):
            at = 128 * (quarter % 2)
            cell = [cells_ref[zh * 8 + a, 2, quarter // 2 : quarter // 2 + 1, at : at + 128] for zh in range(2)]
            cell = jnp.concatenate([jnp.broadcast_to(part, (4, 128)) for part in cell], axis=0).astype(jnp.int32)
            layer = lax.shift_right_logical(cell, 8)
            lane = cell & 127
            upper = (cell & 128) == 128
            found = [
                jnp.where(upper, _lanes_of(tile[:, 128:], lane), _lanes_of(tile[:, :128], lane))
                for tile in tiles
            ]
            sine_at = _lanes_of(weight_ref[group, 0:8, :], layer)
            step_at = _lanes_of(weight_ref[group, 8:16, :], layer)
            for field, term in enumerate((sine_at * found[1], sine_at * found[2], step_at * found[0])):
                term = term + pltpu.roll(term, 2, axis=0)
                accel[field].append(term + pltpu.roll(term, 1, axis=0))
        for field in range(3):
            for slot, dest, first in ((1, (a + 7) % 8, 0), (0, (a + 1) % 8, 2)):
                pair = jnp.concatenate(accel[field][first : first + 2], axis=1)
                row = slot * 3 + field
                for zh in range(2):
                    spot = 4 * zh + 3
                    out_ref[zh * 8 + dest, 6 + row // 2, row % 2 : row % 2 + 1, :] = pair[spot : spot + 1, :]


def pick_kernel(positions_ref, velocities_ref, mass_ref, active_ref, lists_ref, counts_ref, wrap_ref, near_ref):
    wanted = jnp.concatenate([lists_ref[0:1, :], lists_ref[1:2, :]], axis=1)
    total = jnp.zeros((32, 2 * CAP), F32)
    for start in range(0, STARS, CHUNK):
        moving = jnp.concatenate(
            [positions_ref[:, start : start + CHUNK], velocities_ref[:, start : start + CHUNK]], axis=0
        )
        high = moving.astype(BF16).astype(F32)
        rest = moving - high
        middle = rest.astype(BF16).astype(F32)
        low = rest - middle
        plain = jnp.concatenate(
            [
                mass_ref[start : start + CHUNK].astype(F32).reshape(1, CHUNK),
                active_ref[:, start : start + CHUNK].astype(F32),
                jnp.zeros((6, CHUNK), F32),
            ],
            axis=0,
        )
        pad = jnp.zeros((2, CHUNK), F32)
        left = jnp.concatenate([high, pad, middle, pad, low, pad, plain], axis=0).astype(BF16)
        hot = jnp.concatenate([_star_hot(wanted, start), _star_hot(wanted, start + 256)], axis=0)
        total += _dot(left, hot)
    moving = (total[0:6] + total[8:14]) + total[16:22]
    slots = lax.broadcasted_iota(jnp.int32, (1, CAP), 1)
    keep = [jnp.where(slots < counts_ref[:, i : i + 1], 1.0, 0.0) for i in range(2)]
    rows = jnp.concatenate(
        [moving, total[24:25] * jnp.concatenate(keep, axis=1), total[25:26]], axis=0
    )
    down = rows[:, :CAP]
    up = rows[:, CAP:]
    odd = lax.rem(lax.axis_index("az"), 2) == 1
    wrap_ref[...] = jnp.where(odd, up, down)
    near_ref[...] = jnp.where(odd, down, up)


def _sample(fields, layer, angle):
    lanes = layer.shape[1]
    hot = _one_hot(angle, SECTOR)
    both = _dot(fields, hot)
    here = lax.broadcasted_iota(jnp.int32, (HEIGHTS, lanes), 0) == layer
    found = []
    for field in range(3):
        block = both[64 * field : 64 * field + 64] + both[192 + 64 * field : 256 + 64 * field]
        found.append(jnp.sum(jnp.where(here, block, 0.0), axis=0, keepdims=True))
    return found


def _advance(position, velocity, accel, live):
    radius = position[0]
    speed = [
        velocity[0] + live * accel[0],
        velocity[1] + live * (accel[1] / radius),
        velocity[2] + live * accel[2],
    ]
    place = [
        position[0] + live * speed[0],
        position[1] + live * (speed[1] / radius),
        position[2] + live * speed[2],
    ]
    return place + speed


def final_kernel(
    modes_ref, table_ref, far_ref, close_ref, positions_ref, velocities_ref, cells_ref, active_ref,
    grid_ref, state_ref, arrive_ref,
):
    pieces = [modes_ref[group, part] for group in range(16) for part in range(6)]
    modes = jnp.concatenate(pieces, axis=0)
    result = _dot3((table_ref[0:256, :], table_ref[256:512, :]), _split(modes))
    for h in range(HEIGHTS):
        grid_ref[h] = result[h : h + 1, :]
    field_high, field_low = _split(result[64:256])
    fields = jnp.concatenate([field_high, field_low], axis=0)

    sums = []
    for part in range(6, 9):
        total = modes_ref[0, part]
        for group in range(1, 16):
            total = total + modes_ref[group, part]
        sums += [total[0:1], total[1:2]]
    odd = lax.rem(lax.axis_index("az"), 2) == 1
    far = far_ref[...]
    close = close_ref[...]
    for slot in range(2):
        picked = jnp.where(odd, far, close) if slot else jnp.where(odd, close, far)
        state = _advance(
            [picked[i : i + 1] for i in range(3)],
            [picked[i : i + 1] for i in range(3, 6)],
            sums[slot * 3 : slot * 3 + 3],
            picked[7:8],
        )
        keep = picked[6:7] > 0.0
        for row, value in enumerate(state + [picked[6:7]]):
            arrive_ref[row, slot : slot + 1, :] = jnp.where(keep, value, 0.0)

    for start in range(0, STARS, CHUNK):
        lanes = slice(start, start + CHUNK)
        cell = cells_ref[:, lanes]
        accel = _sample(fields, lax.shift_right_logical(cell, 8), cell & 255)
        state = _advance(
            [positions_ref[i : i + 1, lanes] for i in range(3)],
            [velocities_ref[i : i + 1, lanes] for i in range(3)],
            accel,
            active_ref[:, lanes].astype(F32),
        )
        for row in range(6):
            state_ref[row : row + 1, lanes] = state[row]


def _call(kernel, out_shape, name, flops, in_smem=(), in_hbm=(), count=0, scratch=(), limit=48 << 20):
    vmem = pl.BlockSpec(memory_space=pltpu.VMEM)
    smem = pl.BlockSpec(memory_space=pltpu.SMEM)
    hbm = pl.BlockSpec(memory_space=pltpu.HBM)
    outs = jax.tree.map(lambda _: vmem, out_shape)
    return pl.pallas_call(
        kernel,
        out_shape=out_shape,
        in_specs=[smem if i in in_smem else hbm if i in in_hbm else vmem for i in range(count)],
        out_specs=outs,
        scratch_shapes=list(scratch),
        name=name,
        cost_estimate=pl.CostEstimate(flops=flops, bytes_accessed=1 << 20, transcendentals=0),
        compiler_params=pltpu.CompilerParams(vmem_limit_bytes=limit),
    )


def per_device(positions, velocities, masses, cells, active, send_lists, send_counts):
    shape = functools.partial(jax.ShapeDtypeStruct, dtype=F32)
    z_axes, plane_axes = ("zh", "az"), ("y", "c", "x")
    exchange = functools.partial(lax.all_to_all, split_axis=0, concat_axis=0, tiled=True)
    table = _split_np(_trig())
    twist = _twist()
    cell = cells.reshape(1, STARS)
    live = active.reshape(1, STARS)

    layered = _call(
        deposit_kernel,
        shape((16, 3, 2, SECTOR)),
        "deposit",
        10**9,
        in_hbm=(0, 1, 2, 3),
        limit=None,
        count=4,
        scratch=[
            pltpu.VMEM((1, STARS), jnp.int32),
            pltpu.VMEM((STARS,), BF16),
            pltpu.VMEM((2, CAP), jnp.int32),
            pltpu.VMEM((STARS // 128, 128), jnp.int32),
            pltpu.SemaphoreType.DMA((4,)),
        ],
    )(cell, masses, send_lists, cells.reshape(STARS // 128, 128))
    layered, eigen, late_lists = lax.optimization_barrier((layered, jnp.asarray(_eigen()), send_lists))
    sectors = exchange(layered, z_axes)
    factors = _call(
        factor_kernel,
        (shape((64, SECTOR)), shape((64, SECTOR)), shape((64, SECTOR)), shape((8, SECTOR))),
        "factor",
        10**9,
        in_smem=(0,),
        count=1,
    )(eigen)
    wrap, near = _call(pick_kernel, (shape((8, CAP)), shape((8, CAP))), "pick", 10**9, count=6)(
        positions, velocities, masses, live, late_lists, send_counts.reshape(1, 2)
    )
    sectors, factors, wrap, near = lax.optimization_barrier((sectors, factors, wrap, near))
    spectrum = _call(forward_kernel, shape((32, 2, SECTOR)), "forward", 10**9, count=3)(
        sectors, twist, table
    )
    columns = exchange(spectrum, plane_axes)
    solved = _call(
        solve_kernel,
        shape((32, 4, SECTOR)),
        "solve",
        10**9,
        count=5,
        scratch=[pltpu.VMEM((64, SECTOR), F32)],
    )(columns, *factors)
    waves = exchange(solved, plane_axes)
    angles = _call(inverse_kernel, shape((16, 9, 2, SECTOR)), "inverse", 10**9, count=5)(
        waves, twist, table, sectors, _weight_table()
    )
    angles, wrap, near = lax.optimization_barrier((angles, wrap, near))
    modes = exchange(angles, z_axes)
    far = lax.ppermute(wrap, "az", [(i, (i + 1) % 8 if i % 2 else (i + 7) % 8) for i in range(8)])
    close = lax.ppermute(near, "az", [(i, i ^ 1) for i in range(8)])
    potential, state, arrivals = _call(
        final_kernel,
        (shape((64, 1, SECTOR)), shape((6, STARS)), shape((7, 2, CAP))),
        "final",
        10**9,
        count=8,
    )(modes, _split_np(_field_table()), far, close, positions, velocities, cell, live)
    return potential, state, arrivals.transpose(1, 0, 2)


def solution(mesh):
    fine = Mesh(mesh.devices.reshape(8, 4, 2, 4, 2), ("az", "x", "zh", "y", "c"))
    rz = ("x", "zh", "y", "c")
    every = ("az",) + rz
    return jax.shard_map(
        per_device,
        mesh=fine,
        in_specs=(
            P(None, every),
            P(None, every),
            P(every),
            P(every),
            P(every),
            P(None, every),
            P(None, every),
        ),
        out_specs=(P(None, rz, "az"), P(None, every), P(None, None, every)),
        check_vma=False,
    )
```

```python
import functools
import math

import jax
import jax.numpy as jnp
import numpy as np
from jax import lax
from jax.experimental import pallas as pl
from jax.experimental.pallas import tpu as pltpu
from jax.sharding import Mesh
from jax.sharding import PartitionSpec as P

HEIGHTS = 64
RADII = 64
AZIM = 2048
SECTOR = 256
STARS = 4096
CAP = 256
CHUNK = 512
INNER = 8.0

F32 = jnp.float32
BF16 = jnp.bfloat16


PLANE = ("y1", "x1", "c", "y0", "x0")


def _split_np(table):
    exact = np.asarray(table, np.float64)
    high = exact.astype(np.float32).astype(jnp.bfloat16)
    low = (exact - high.astype(np.float64)).astype(np.float32).astype(jnp.bfloat16)
    return np.concatenate([high, low], axis=0)


def _sine():
    levels = np.arange(HEIGHTS) + 1
    turns = levels[:, None] * levels[None, :] % (2 * (HEIGHTS + 1))
    return math.sqrt(2.0 / (HEIGHTS + 1)) * np.sin(turns * (math.pi / (HEIGHTS + 1)))


def _trig():
    ids = np.arange(SECTOR)
    theta = (ids[:, None] * ids[None, :] % SECTOR) * (2.0 * math.pi / SECTOR)
    return np.concatenate([np.cos(theta), np.sin(theta)], axis=0)


def _twist():
    residues = np.arange(8)
    angles = np.arange(AZIM)
    theta = (residues[:, None] * angles[None, :] % AZIM) * (2.0 * math.pi / AZIM)
    plus = np.cos(theta) + np.sin(theta)
    minus = np.cos(theta) - np.sin(theta)
    return np.concatenate([plus, minus], axis=0).reshape(128, SECTOR).astype(np.float32)


def _field_table():
    sine = _sine()
    shifted = np.zeros((HEIGHTS, HEIGHTS))
    shifted[:-1] += sine[1:]
    shifted[1:] -= sine[:-1]
    vertical = 0.5 * shifted
    table = np.zeros((4, HEIGHTS, 16, 3, 4))
    by_group = sine.reshape(HEIGHTS, 16, 4)
    table[0, :, :, 0, :] = by_group
    table[1, :, :, 1, :] = -by_group
    table[2, :, :, 2, :] = -by_group
    table[3, :, :, 0, :] = -vertical.reshape(HEIGHTS, 16, 4)
    return table.reshape(4 * HEIGHTS, 192) / AZIM


def _weight_table():
    table = _field_table().reshape(4, HEIGHTS, 16, 3, 4)
    exact = np.zeros((16, 2, 2, 4, 128), np.float32)
    exact[:, 0, :, :, :HEIGHTS] = table[1, :, :, 1, :].transpose(1, 2, 0)[:, None]
    exact[:, 1, :, :, :HEIGHTS] = table[3, :, :, 0, :].transpose(1, 2, 0)[:, None]
    return exact.reshape(16, 16, 128)


def _eigen():
    levels = np.arange(HEIGHTS) + 1.0
    return ((2.0 * np.sin(levels * (math.pi / (2 * (HEIGHTS + 1))))) ** 2).astype(np.float32)


def _row_of(radius):
    bits = {name: (radius >> (5 - i)) & 1 for i, name in enumerate(("x1", "x0", "zh", "y1", "y0", "c"))}
    row = 0
    for name in PLANE + ("zh",):
        row = row * 2 + bits[name]
    return row


def _split(value):
    high = value.astype(BF16)
    low = (value - high.astype(F32)).astype(BF16)
    return high, low


def _dot(a, b):
    return jnp.dot(a, b, preferred_element_type=F32)


def _dot3(a, b):
    (a_high, a_low), (b_high, b_low) = a, b
    return _dot(a_high, b_high) + (_dot(a_low, b_high) + _dot(a_high, b_low))


def _rows(rows, lanes):
    return lax.broadcasted_iota(jnp.int32, (rows, lanes), 0).astype(F32).astype(BF16)


def _one_hot(ids, rows):
    lanes = ids.shape[1]
    small = jnp.broadcast_to(ids.astype(F32).astype(BF16), (rows, lanes))
    here = _rows(rows, lanes) == small
    return jnp.where(here, jnp.ones((), BF16), jnp.zeros((), BF16))


def _star_hot(wanted, start):
    offset = wanted - start
    inside = (offset >= 0) & (offset < 256)
    return _one_hot(jnp.where(inside, offset, -1), 256)


def _sine_in_kernel():
    shape = (HEIGHTS, HEIGHTS)
    first = lax.broadcasted_iota(jnp.int32, shape, 0) + 1
    second = lax.broadcasted_iota(jnp.int32, shape, 1) + 1
    turns = lax.rem(first * second, 2 * (HEIGHTS + 1))
    negative = turns > HEIGHTS + 1
    turns = jnp.where(negative, turns - (HEIGHTS + 1), turns)
    turns = jnp.minimum(turns, HEIGHTS + 1 - turns).astype(F32)
    angle = turns * (math.pi / (HEIGHTS + 1))
    square = angle * angle
    series = jnp.full(shape, 1.0 / math.factorial(13), F32)
    for power in (11, 9, 7, 5, 3, 1):
        sign = -1.0 if power % 4 == 3 else 1.0
        series = series * square + sign / math.factorial(power)
    value = series * angle * math.sqrt(2.0 / (HEIGHTS + 1))
    return jnp.where(negative, -value, value)


def _lanes_of(table, ids):
    return jnp.take_along_axis(table, ids, axis=1)


def deposit_kernel(cells_hbm, mass_hbm, lists_hbm, square_hbm, out_ref, cells_ref, mass_ref, lists_ref, square_ref, sems):
    cells_copy = pltpu.make_async_copy(cells_hbm, cells_ref, sems.at[0])
    mass_copy = pltpu.make_async_copy(mass_hbm, mass_ref, sems.at[1])
    lists_copy = pltpu.make_async_copy(lists_hbm, lists_ref, sems.at[2])
    cells_copy.start()
    square_copy = pltpu.make_async_copy(square_hbm, square_ref, sems.at[3])
    lists_copy.start()
    mass_copy.start()
    square_copy.start()
    sine = _split(_sine_in_kernel())
    cells_copy.wait()
    lists_copy.wait()
    mass_copy.wait()
    square_copy.wait()
    wanted = [lists_ref[i : i + 1, half : half + 128] for i in range(2) for half in (0, 128)]
    wanted = jnp.concatenate(wanted + wanted, axis=0)
    lane = wanted & 127
    line = lax.shift_right_logical(wanted, 7)
    sent = jnp.zeros((8, 128), jnp.int32)
    for row in range(STARS // 128):
        found = _lanes_of(jnp.broadcast_to(square_ref[row : row + 1, :], (8, 128)), lane)
        sent = jnp.where(line == row, found, sent)
    sent = sent.astype(F32)
    total = jnp.zeros((HEIGHTS, SECTOR), F32)
    for start in range(0, STARS, CHUNK):
        cell = cells_ref[:, start : start + CHUNK]
        mass = mass_ref[start : start + CHUNK].astype(F32).reshape(1, CHUNK)
        layer = lax.shift_right_logical(cell, 8)
        angle = cell & 255
        here = lax.broadcasted_iota(jnp.int32, (HEIGHTS, CHUNK), 0) == layer
        left = jnp.where(here, mass, 0.0).astype(BF16)
        right = _one_hot(angle, SECTOR)
        total += lax.dot_general(
            left, right, (((1,), (1,)), ((), ())), preferred_element_type=F32
        )
    layered = _dot3(sine, _split(total))
    cells_sent = [jnp.concatenate([sent[2 * i : 2 * i + 1], sent[2 * i + 1 : 2 * i + 2]], axis=1) for i in range(2)]
    for group in range(16):
        out_ref[group, 0] = layered[4 * group : 4 * group + 2, :]
        out_ref[group, 1] = layered[4 * group + 2 : 4 * group + 4, :]
        out_ref[group, 2, 0:1, :] = cells_sent[0]
        out_ref[group, 2, 1:2, :] = cells_sent[1]


def forward_kernel(x_ref, twist_ref, table_ref, out_ref):
    tiles = []
    for a in range(8):
        parts = [x_ref[zh * 8 + a, half] for zh in range(2) for half in range(2)]
        tiles.append(jnp.concatenate(parts, axis=0))
    rows = []
    for n2 in range(8):
        even = None
        odd = None
        for a in range(8):
            at = 8 * n2 + a
            plus = tiles[a] * twist_ref[at : at + 1, :]
            minus = tiles[a] * twist_ref[64 + at : 65 + at, :]
            even = plus if even is None else even + plus
            odd = minus if odd is None else odd + minus
        rows.append(jnp.concatenate([even, odd], axis=1))
    left = _split(jnp.concatenate(rows, axis=0))
    result = _dot3(left, (table_ref[0:512, :], table_ref[512:1024, :]))
    for n2 in range(8):
        for k in range(4):
            for zh in range(2):
                at = n2 * 8 + zh * 4 + k
                out_ref[n2 * 4 + k, zh : zh + 1, :] = result[at : at + 1, :]


def factor_kernel(eigen_ref, inverse_ref, carry_ref, factor_ref, joint_ref):
    group = lax.axis_index("zh") * 8 + lax.axis_index("az")
    place = 0
    for name in PLANE:
        place = place * 2 + lax.axis_index(name)
    level = group * 4 + lax.rem(place, 4)
    residue = lax.div(place, 4)
    eigen = eigen_ref[level]
    mode = lax.broadcasted_iota(jnp.int32, (1, SECTOR), 1) * 8 + residue
    mode = jnp.minimum(mode, AZIM - mode).astype(F32)
    square = mode * mode
    top = None
    bottom = None
    for step in range(RADII // 2):
        i = step
        radius = INNER + i + 0.5
        lower = -(radius - 0.5) / radius
        upper = -(radius + 0.5) / radius
        denom = (2.0 + eigen) + square * (1.0 / (radius * radius))
        if top is not None:
            denom = denom - lower * top
        inverse = 1.0 / denom
        top = upper * inverse
        row = _row_of(i)
        inverse_ref[row : row + 1, :] = -inverse
        carry_ref[row : row + 1, :] = -lower * inverse
        factor_ref[row : row + 1, :] = -top
        i = RADII - 1 - step
        radius = INNER + i + 0.5
        lower = -(radius - 0.5) / radius
        upper = -(radius + 0.5) / radius
        denom = (2.0 + eigen) + square * (1.0 / (radius * radius))
        if bottom is not None:
            denom = denom - upper * bottom
        inverse = 1.0 / denom
        bottom = lower * inverse
        row = _row_of(i)
        inverse_ref[row : row + 1, :] = -inverse
        carry_ref[row : row + 1, :] = -upper * inverse
        factor_ref[row : row + 1, :] = -bottom
    joint_ref[...] = jnp.broadcast_to(1.0 / (1.0 - top * bottom), (8, SECTOR))


def solve_kernel(source_ref, inverse_ref, carry_ref, factor_ref, joint_ref, out_ref, scaled_ref):
    half = RADII // 2
    for place in range(32):
        rows = slice(2 * place, 2 * place + 2)
        scaled_ref[rows, :] = source_ref[place] * inverse_ref[rows, :]

    def at(ref, i):
        row = _row_of(i)
        return ref[row : row + 1, :]

    values = [None] * RADII
    values[0] = at(scaled_ref, 0)
    values[RADII - 1] = at(scaled_ref, RADII - 1)
    for step in range(1, half):
        i = step
        values[i] = at(scaled_ref, i) + at(carry_ref, i) * values[i - 1]
        i = RADII - 1 - step
        values[i] = at(scaled_ref, i) + at(carry_ref, i) * values[i + 1]
    solved = [None] * RADII
    solved[half - 1] = (values[half - 1] + at(factor_ref, half - 1) * values[half]) * joint_ref[0:1, :]
    solved[half] = values[half] + at(factor_ref, half) * solved[half - 1]
    for step in range(1, half):
        i = half - 1 - step
        solved[i] = values[i] + at(factor_ref, i) * solved[i + 1]
        i = half + step
        solved[i] = values[i] + at(factor_ref, i) * solved[i - 1]
    for i in range(RADII):
        row = _row_of(i)
        place, zh = row >> 1, row & 1
        out_ref[place, zh : zh + 1, :] = solved[i]
        if i == 0:
            slope = solved[1] * 0.5
        elif i == RADII - 1:
            slope = solved[RADII - 2] * -0.5
        else:
            slope = (solved[i + 1] - solved[i - 1]) * 0.5
        out_ref[place, zh + 2 : zh + 3, :] = slope


def inverse_kernel(x_ref, twist_ref, table_ref, cells_ref, weight_ref, out_ref):
    group = lax.axis_index("zh") * 8 + lax.axis_index("az")
    fields = [[], [], []]
    for n2 in range(8):
        pair = []
        for field in range(2):
            spots = [(n2 * 4 + k, field * 2 + zh) for zh in range(2) for k in range(4)]
            pair.append(jnp.concatenate([x_ref[at, row : row + 1, :] for at, row in spots], axis=0))
        mode = lax.broadcasted_iota(jnp.int32, (8, SECTOR), 1) * 8 + n2
        signed = jnp.where(2 * mode < AZIM, mode, mode - AZIM)
        signed = jnp.where(2 * mode == AZIM, 0, signed).astype(F32)
        fields[0].append(pair[0])
        fields[1].append(pair[1])
        fields[2].append(pair[0] * signed)
    cosine = (table_ref[0:256, :], table_ref[512:768, :])
    sine = (table_ref[256:512, :], table_ref[768:1024, :])
    waves = []
    for field in range(3):
        left = _split(jnp.concatenate(fields[field], axis=0))
        waves.append((_dot3(left, cosine), _dot3(left, sine)))
    for a in range(8):
        tiles = []
        for field in range(3):
            total = None
            for n2 in range(8):
                even = waves[field][0][8 * n2 : 8 * n2 + 8, :]
                odd = waves[field][1][8 * n2 : 8 * n2 + 8, :]
                plus = twist_ref[8 * n2 + a : 8 * n2 + a + 1, :]
                minus = twist_ref[64 + 8 * n2 + a : 65 + 8 * n2 + a, :]
                if field < 2:
                    term = even * plus + odd * minus
                else:
                    term = even * minus - odd * plus
                total = term if total is None else total + term
            for zh in range(2):
                for half in range(2):
                    row = zh * 4 + half * 2
                    out_ref[zh * 8 + a, field * 2 + half] = total[row : row + 2, :]
            tiles.append(total)
        accel = [[], [], []]
        for quarter in range(4):
            at = 128 * (quarter % 2)
            cell = [cells_ref[zh * 8 + a, 2, quarter // 2 : quarter // 2 + 1, at : at + 128] for zh in range(2)]
            cell = jnp.concatenate([jnp.broadcast_to(part, (4, 128)) for part in cell], axis=0).astype(jnp.int32)
            layer = lax.shift_right_logical(cell, 8)
            lane = cell & 127
            upper = (cell & 128) == 128
            found = [
                jnp.where(upper, _lanes_of(tile[:, 128:], lane), _lanes_of(tile[:, :128], lane))
                for tile in tiles
            ]
            sine_at = _lanes_of(weight_ref[group, 0:8, :], layer)
            step_at = _lanes_of(weight_ref[group, 8:16, :], layer)
            for field, term in enumerate((sine_at * found[1], sine_at * found[2], step_at * found[0])):
                term = term + pltpu.roll(term, 2, axis=0)
                accel[field].append(term + pltpu.roll(term, 1, axis=0))
        for field in range(3):
            for slot, dest, first in ((1, (a + 7) % 8, 0), (0, (a + 1) % 8, 2)):
                pair = jnp.concatenate(accel[field][first : first + 2], axis=1)
                row = slot * 3 + field
                for zh in range(2):
                    spot = 4 * zh + 3
                    out_ref[zh * 8 + dest, 6 + row // 2, row % 2 : row % 2 + 1, :] = pair[spot : spot + 1, :]


def pick_kernel(positions_ref, velocities_ref, mass_ref, active_ref, lists_ref, counts_ref, wrap_ref, near_ref):
    wanted = jnp.concatenate([lists_ref[0:1, :], lists_ref[1:2, :]], axis=1)
    total = jnp.zeros((32, 2 * CAP), F32)
    for start in range(0, STARS, CHUNK):
        moving = jnp.concatenate(
            [positions_ref[:, start : start + CHUNK], velocities_ref[:, start : start + CHUNK]], axis=0
        )
        high = moving.astype(BF16).astype(F32)
        rest = moving - high
        middle = rest.astype(BF16).astype(F32)
        low = rest - middle
        plain = jnp.concatenate(
            [
                mass_ref[start : start + CHUNK].astype(F32).reshape(1, CHUNK),
                active_ref[:, start : start + CHUNK].astype(F32),
                jnp.zeros((6, CHUNK), F32),
            ],
            axis=0,
        )
        pad = jnp.zeros((2, CHUNK), F32)
        left = jnp.concatenate([high, pad, middle, pad, low, pad, plain], axis=0).astype(BF16)
        hot = jnp.concatenate([_star_hot(wanted, start), _star_hot(wanted, start + 256)], axis=0)
        total += _dot(left, hot)
    moving = (total[0:6] + total[8:14]) + total[16:22]
    slots = lax.broadcasted_iota(jnp.int32, (1, CAP), 1)
    keep = [jnp.where(slots < counts_ref[:, i : i + 1], 1.0, 0.0) for i in range(2)]
    rows = jnp.concatenate(
        [moving, total[24:25] * jnp.concatenate(keep, axis=1), total[25:26]], axis=0
    )
    down = rows[:, :CAP]
    up = rows[:, CAP:]
    odd = lax.rem(lax.axis_index("az"), 2) == 1
    wrap_ref[...] = jnp.where(odd, up, down)
    near_ref[...] = jnp.where(odd, down, up)


def _sample(fields, layer, angle):
    lanes = layer.shape[1]
    hot = _one_hot(angle, SECTOR)
    both = _dot(fields, hot)
    here = lax.broadcasted_iota(jnp.int32, (HEIGHTS, lanes), 0) == layer
    found = []
    for field in range(3):
        block = both[64 * field : 64 * field + 64] + both[192 + 64 * field : 256 + 64 * field]
        found.append(jnp.sum(jnp.where(here, block, 0.0), axis=0, keepdims=True))
    return found


def _advance(position, velocity, accel, live):
    radius = position[0]
    speed = [
        velocity[0] + live * accel[0],
        velocity[1] + live * (accel[1] / radius),
        velocity[2] + live * accel[2],
    ]
    place = [
        position[0] + live * speed[0],
        position[1] + live * (speed[1] / radius),
        position[2] + live * speed[2],
    ]
    return place + speed


def final_kernel(
    modes_ref, table_ref, close_ref, far_ref, positions_ref, velocities_ref, cells_ref, active_ref,
    grid_ref, state_ref, arrive_ref,
):
    pieces = [modes_ref[group, part] for group in range(16) for part in range(6)]
    modes = jnp.concatenate(pieces, axis=0)
    result = _dot3((table_ref[0:256, :], table_ref[256:512, :]), _split(modes))
    for h in range(HEIGHTS):
        grid_ref[h] = result[h : h + 1, :]
    field_high, field_low = _split(result[64:256])
    fields = jnp.concatenate([field_high, field_low], axis=0)

    sums = []
    for part in range(6, 9):
        total = modes_ref[0, part]
        for group in range(1, 16):
            total = total + modes_ref[group, part]
        sums += [total[0:1], total[1:2]]
    odd = lax.rem(lax.axis_index("az"), 2) == 1
    far = far_ref[...]
    close = close_ref[...]
    for slot in range(2):
        picked = jnp.where(odd, far, close) if slot else jnp.where(odd, close, far)
        state = _advance(
            [picked[i : i + 1] for i in range(3)],
            [picked[i : i + 1] for i in range(3, 6)],
            sums[slot * 3 : slot * 3 + 3],
            picked[7:8],
        )
        keep = picked[6:7] > 0.0
        for row, value in enumerate(state + [picked[6:7]]):
            arrive_ref[row, slot : slot + 1, :] = jnp.where(keep, value, 0.0)

    for start in range(0, STARS, CHUNK):
        lanes = slice(start, start + CHUNK)
        cell = cells_ref[:, lanes]
        accel = _sample(fields, lax.shift_right_logical(cell, 8), cell & 255)
        state = _advance(
            [positions_ref[i : i + 1, lanes] for i in range(3)],
            [velocities_ref[i : i + 1, lanes] for i in range(3)],
            accel,
            active_ref[:, lanes].astype(F32),
        )
        for row in range(6):
            state_ref[row : row + 1, lanes] = state[row]


def _call(kernel, out_shape, name, flops, in_smem=(), in_hbm=(), count=0, scratch=(), limit=48 << 20):
    vmem = pl.BlockSpec(memory_space=pltpu.VMEM)
    smem = pl.BlockSpec(memory_space=pltpu.SMEM)
    hbm = pl.BlockSpec(memory_space=pltpu.HBM)
    outs = jax.tree.map(lambda _: vmem, out_shape)
    return pl.pallas_call(
        kernel,
        out_shape=out_shape,
        in_specs=[smem if i in in_smem else hbm if i in in_hbm else vmem for i in range(count)],
        out_specs=outs,
        scratch_shapes=list(scratch),
        name=name,
        cost_estimate=pl.CostEstimate(flops=flops, bytes_accessed=1 << 20, transcendentals=0),
        compiler_params=pltpu.CompilerParams(vmem_limit_bytes=limit),
    )


def per_device(positions, velocities, masses, cells, active, send_lists, send_counts):
    shape = functools.partial(jax.ShapeDtypeStruct, dtype=F32)
    z_axes, plane_axes = ("zh", "az"), PLANE
    exchange = functools.partial(lax.all_to_all, split_axis=0, concat_axis=0, tiled=True)
    table = _split_np(_trig())
    twist = _twist()
    cell = cells.reshape(1, STARS)
    live = active.reshape(1, STARS)

    layered = _call(
        deposit_kernel,
        shape((16, 3, 2, SECTOR)),
        "deposit",
        10**9,
        in_hbm=(0, 1, 2, 3),
        limit=None,
        count=4,
        scratch=[
            pltpu.VMEM((1, STARS), jnp.int32),
            pltpu.VMEM((STARS,), BF16),
            pltpu.VMEM((2, CAP), jnp.int32),
            pltpu.VMEM((STARS // 128, 128), jnp.int32),
            pltpu.SemaphoreType.DMA((4,)),
        ],
    )(cell, masses, send_lists, cells.reshape(STARS // 128, 128))
    layered, eigen, late_lists = lax.optimization_barrier((layered, jnp.asarray(_eigen()), send_lists))
    sectors = exchange(layered, z_axes)
    factors = _call(
        factor_kernel,
        (shape((64, SECTOR)), shape((64, SECTOR)), shape((64, SECTOR)), shape((8, SECTOR))),
        "factor",
        10**9,
        in_smem=(0,),
        count=1,
    )(eigen)
    wrap, near = _call(pick_kernel, (shape((8, CAP)), shape((8, CAP))), "pick", 10**9, count=6)(
        positions, velocities, masses, live, late_lists, send_counts.reshape(1, 2)
    )
    sectors, factors, wrap, near = lax.optimization_barrier((sectors, factors, wrap, near))
    spectrum = _call(forward_kernel, shape((32, 2, SECTOR)), "forward", 10**9, count=3)(
        sectors, twist, table
    )
    columns = exchange(spectrum, plane_axes)
    solved = _call(
        solve_kernel,
        shape((32, 4, SECTOR)),
        "solve",
        10**9,
        count=5,
        scratch=[pltpu.VMEM((64, SECTOR), F32)],
    )(columns, *factors)
    waves = exchange(solved, plane_axes)
    angles = _call(inverse_kernel, shape((16, 9, 2, SECTOR)), "inverse", 10**9, count=5)(
        waves, twist, table, sectors, _weight_table()
    )
    angles, wrap, near = lax.optimization_barrier((angles, wrap, near))
    modes = exchange(angles, z_axes)
    close = lax.ppermute(near, "az", [(i, i ^ 1) for i in range(8)])
    far = lax.ppermute(wrap, "az", [(i, (i + 1) % 8 if i % 2 else (i + 7) % 8) for i in range(8)])
    potential, state, arrivals = _call(
        final_kernel,
        (shape((64, 1, SECTOR)), shape((6, STARS)), shape((7, 2, CAP))),
        "final",
        10**9,
        count=8,
    )(modes, _split_np(_field_table()), close, far, positions, velocities, cell, live)
    return potential, state, arrivals.transpose(1, 0, 2)


def solution(mesh):
    fine = Mesh(mesh.devices.reshape(8, 2, 2, 2, 2, 2, 2), ("az", "x1", "x0", "zh", "y1", "y0", "c"))
    rz = ("x1", "x0", "zh", "y1", "y0", "c")
    every = ("az",) + rz
    return jax.shard_map(
        per_device,
        mesh=fine,
        in_specs=(
            P(None, every),
            P(None, every),
            P(every),
            P(every),
            P(every),
            P(None, every),
            P(None, every),
        ),
        out_specs=(P(None, rz, "az"), P(None, every), P(None, None, every)),
        check_vma=False,
    )
```

```python
import functools
import math

import jax
import jax.numpy as jnp
import numpy as np
from jax import lax
from jax.experimental import pallas as pl
from jax.experimental.pallas import tpu as pltpu
from jax.sharding import Mesh
from jax.sharding import PartitionSpec as P

HEIGHTS = 64
RADII = 64
AZIM = 2048
SECTOR = 256
STARS = 4096
CAP = 256
CHUNK = 512
INNER = 8.0

F32 = jnp.float32
BF16 = jnp.bfloat16


AZ = ("a2", "a1", "a0")
PLANE = ("y1", "x1", "c", "y0", "x0")
ORDER = ("zh", "a2", "a0", "a1")


def _group(a, zh):
    bits = {"zh": zh, "a2": a >> 2, "a1": (a >> 1) & 1, "a0": a & 1}
    place = 0
    for name in ORDER:
        place = place * 2 + bits[name]
    return place


def _own_group():
    place = 0
    for name in ORDER:
        place = place * 2 + lax.axis_index(name)
    return place


def _split_np(table):
    exact = np.asarray(table, np.float64)
    high = exact.astype(np.float32).astype(jnp.bfloat16)
    low = (exact - high.astype(np.float64)).astype(np.float32).astype(jnp.bfloat16)
    return np.concatenate([high, low], axis=0)


def _sine():
    levels = np.arange(HEIGHTS) + 1
    turns = levels[:, None] * levels[None, :] % (2 * (HEIGHTS + 1))
    return math.sqrt(2.0 / (HEIGHTS + 1)) * np.sin(turns * (math.pi / (HEIGHTS + 1)))


def _trig():
    ids = np.arange(SECTOR)
    theta = (ids[:, None] * ids[None, :] % SECTOR) * (2.0 * math.pi / SECTOR)
    return np.concatenate([np.cos(theta), np.sin(theta)], axis=0)


def _twist():
    residues = np.arange(8)
    angles = np.arange(AZIM)
    theta = (residues[:, None] * angles[None, :] % AZIM) * (2.0 * math.pi / AZIM)
    plus = np.cos(theta) + np.sin(theta)
    minus = np.cos(theta) - np.sin(theta)
    return np.concatenate([plus, minus], axis=0).reshape(128, SECTOR).astype(np.float32)


def _field_table():
    sine = _sine()
    shifted = np.zeros((HEIGHTS, HEIGHTS))
    shifted[:-1] += sine[1:]
    shifted[1:] -= sine[:-1]
    vertical = 0.5 * shifted
    table = np.zeros((4, HEIGHTS, 16, 3, 4))
    by_group = sine.reshape(HEIGHTS, 16, 4)
    table[0, :, :, 0, :] = by_group
    table[1, :, :, 1, :] = -by_group
    table[2, :, :, 2, :] = -by_group
    table[3, :, :, 0, :] = -vertical.reshape(HEIGHTS, 16, 4)
    return table.reshape(4 * HEIGHTS, 192) / AZIM


def _weight_table():
    table = _field_table().reshape(4, HEIGHTS, 16, 3, 4)
    exact = np.zeros((16, 2, 2, 4, 128), np.float32)
    exact[:, 0, :, :, :HEIGHTS] = table[1, :, :, 1, :].transpose(1, 2, 0)[:, None]
    exact[:, 1, :, :, :HEIGHTS] = table[3, :, :, 0, :].transpose(1, 2, 0)[:, None]
    return exact.reshape(16, 16, 128)


def _eigen():
    levels = np.arange(HEIGHTS) + 1.0
    return ((2.0 * np.sin(levels * (math.pi / (2 * (HEIGHTS + 1))))) ** 2).astype(np.float32)


def _row_of(radius):
    bits = {name: (radius >> (5 - i)) & 1 for i, name in enumerate(("x1", "x0", "zh", "y1", "y0", "c"))}
    row = 0
    for name in PLANE + ("zh",):
        row = row * 2 + bits[name]
    return row


def _split(value):
    high = value.astype(BF16)
    low = (value - high.astype(F32)).astype(BF16)
    return high, low


def _dot(a, b):
    return jnp.dot(a, b, preferred_element_type=F32)


def _dot3(a, b):
    (a_high, a_low), (b_high, b_low) = a, b
    return _dot(a_high, b_high) + (_dot(a_low, b_high) + _dot(a_high, b_low))


def _rows(rows, lanes):
    return lax.broadcasted_iota(jnp.int32, (rows, lanes), 0).astype(F32).astype(BF16)


def _one_hot(ids, rows):
    lanes = ids.shape[1]
    small = jnp.broadcast_to(ids.astype(F32).astype(BF16), (rows, lanes))
    here = _rows(rows, lanes) == small
    return jnp.where(here, jnp.ones((), BF16), jnp.zeros((), BF16))


def _star_hot(wanted, start):
    offset = wanted - start
    inside = (offset >= 0) & (offset < 256)
    return _one_hot(jnp.where(inside, offset, -1), 256)


def _sine_in_kernel():
    shape = (HEIGHTS, HEIGHTS)
    first = lax.broadcasted_iota(jnp.int32, shape, 0) + 1
    second = lax.broadcasted_iota(jnp.int32, shape, 1) + 1
    turns = lax.rem(first * second, 2 * (HEIGHTS + 1))
    negative = turns > HEIGHTS + 1
    turns = jnp.where(negative, turns - (HEIGHTS + 1), turns)
    turns = jnp.minimum(turns, HEIGHTS + 1 - turns).astype(F32)
    angle = turns * (math.pi / (HEIGHTS + 1))
    square = angle * angle
    series = jnp.full(shape, 1.0 / math.factorial(13), F32)
    for power in (11, 9, 7, 5, 3, 1):
        sign = -1.0 if power % 4 == 3 else 1.0
        series = series * square + sign / math.factorial(power)
    value = series * angle * math.sqrt(2.0 / (HEIGHTS + 1))
    return jnp.where(negative, -value, value)


def _lanes_of(table, ids):
    return jnp.take_along_axis(table, ids, axis=1)


def deposit_kernel(cells_hbm, mass_hbm, lists_hbm, square_hbm, out_ref, cells_ref, mass_ref, lists_ref, square_ref, sems):
    cells_copy = pltpu.make_async_copy(cells_hbm, cells_ref, sems.at[0])
    mass_copy = pltpu.make_async_copy(mass_hbm, mass_ref, sems.at[1])
    lists_copy = pltpu.make_async_copy(lists_hbm, lists_ref, sems.at[2])
    cells_copy.start()
    square_copy = pltpu.make_async_copy(square_hbm, square_ref, sems.at[3])
    lists_copy.start()
    mass_copy.start()
    square_copy.start()
    sine = _split(_sine_in_kernel())
    cells_copy.wait()
    lists_copy.wait()
    mass_copy.wait()
    square_copy.wait()
    wanted = [lists_ref[i : i + 1, half : half + 128] for i in range(2) for half in (0, 128)]
    wanted = jnp.concatenate(wanted + wanted, axis=0)
    lane = wanted & 127
    line = lax.shift_right_logical(wanted, 7)
    sent = jnp.zeros((8, 128), jnp.int32)
    for row in range(STARS // 128):
        found = _lanes_of(jnp.broadcast_to(square_ref[row : row + 1, :], (8, 128)), lane)
        sent = jnp.where(line == row, found, sent)
    sent = sent.astype(F32)
    total = jnp.zeros((HEIGHTS, SECTOR), F32)
    for start in range(0, STARS, CHUNK):
        cell = cells_ref[:, start : start + CHUNK]
        mass = mass_ref[start : start + CHUNK].astype(F32).reshape(1, CHUNK)
        layer = lax.shift_right_logical(cell, 8)
        angle = cell & 255
        here = lax.broadcasted_iota(jnp.int32, (HEIGHTS, CHUNK), 0) == layer
        left = jnp.where(here, mass, 0.0).astype(BF16)
        right = _one_hot(angle, SECTOR)
        total += lax.dot_general(
            left, right, (((1,), (1,)), ((), ())), preferred_element_type=F32
        )
    layered = _dot3(sine, _split(total))
    cells_sent = [jnp.concatenate([sent[2 * i : 2 * i + 1], sent[2 * i + 1 : 2 * i + 2]], axis=1) for i in range(2)]
    for group in range(16):
        out_ref[group, 0] = layered[4 * group : 4 * group + 2, :]
        out_ref[group, 1] = layered[4 * group + 2 : 4 * group + 4, :]
        out_ref[group, 2, 0:1, :] = cells_sent[0]
        out_ref[group, 2, 1:2, :] = cells_sent[1]


def forward_kernel(x_ref, twist_ref, table_ref, out_ref):
    tiles = []
    for a in range(8):
        parts = [x_ref[_group(a, zh), half] for zh in range(2) for half in range(2)]
        tiles.append(jnp.concatenate(parts, axis=0))
    rows = []
    for n2 in range(8):
        even = None
        odd = None
        for a in range(8):
            at = 8 * n2 + a
            plus = tiles[a] * twist_ref[at : at + 1, :]
            minus = tiles[a] * twist_ref[64 + at : 65 + at, :]
            even = plus if even is None else even + plus
            odd = minus if odd is None else odd + minus
        rows.append(jnp.concatenate([even, odd], axis=1))
    left = _split(jnp.concatenate(rows, axis=0))
    result = _dot3(left, (table_ref[0:512, :], table_ref[512:1024, :]))
    for n2 in range(8):
        for k in range(4):
            for zh in range(2):
                at = n2 * 8 + zh * 4 + k
                out_ref[n2 * 4 + k, zh : zh + 1, :] = result[at : at + 1, :]


def factor_kernel(eigen_ref, inverse_ref, carry_ref, factor_ref, joint_ref):
    group = _own_group()
    place = 0
    for name in PLANE:
        place = place * 2 + lax.axis_index(name)
    level = group * 4 + lax.rem(place, 4)
    residue = lax.div(place, 4)
    eigen = eigen_ref[level]
    mode = lax.broadcasted_iota(jnp.int32, (1, SECTOR), 1) * 8 + residue
    mode = jnp.minimum(mode, AZIM - mode).astype(F32)
    square = mode * mode
    top = None
    bottom = None
    for step in range(RADII // 2):
        i = step
        radius = INNER + i + 0.5
        lower = -(radius - 0.5) / radius
        upper = -(radius + 0.5) / radius
        denom = (2.0 + eigen) + square * (1.0 / (radius * radius))
        if top is not None:
            denom = denom - lower * top
        inverse = 1.0 / denom
        top = upper * inverse
        row = _row_of(i)
        inverse_ref[row : row + 1, :] = -inverse
        carry_ref[row : row + 1, :] = -lower * inverse
        factor_ref[row : row + 1, :] = -top
        i = RADII - 1 - step
        radius = INNER + i + 0.5
        lower = -(radius - 0.5) / radius
        upper = -(radius + 0.5) / radius
        denom = (2.0 + eigen) + square * (1.0 / (radius * radius))
        if bottom is not None:
            denom = denom - upper * bottom
        inverse = 1.0 / denom
        bottom = lower * inverse
        row = _row_of(i)
        inverse_ref[row : row + 1, :] = -inverse
        carry_ref[row : row + 1, :] = -upper * inverse
        factor_ref[row : row + 1, :] = -bottom
    joint_ref[...] = jnp.broadcast_to(1.0 / (1.0 - top * bottom), (8, SECTOR))


def solve_kernel(source_ref, inverse_ref, carry_ref, factor_ref, joint_ref, out_ref, scaled_ref):
    half = RADII // 2
    for place in range(32):
        rows = slice(2 * place, 2 * place + 2)
        scaled_ref[rows, :] = source_ref[place] * inverse_ref[rows, :]

    def at(ref, i):
        row = _row_of(i)
        return ref[row : row + 1, :]

    values = [None] * RADII
    values[0] = at(scaled_ref, 0)
    values[RADII - 1] = at(scaled_ref, RADII - 1)
    for step in range(1, half):
        i = step
        values[i] = at(scaled_ref, i) + at(carry_ref, i) * values[i - 1]
        i = RADII - 1 - step
        values[i] = at(scaled_ref, i) + at(carry_ref, i) * values[i + 1]
    solved = [None] * RADII
    solved[half - 1] = (values[half - 1] + at(factor_ref, half - 1) * values[half]) * joint_ref[0:1, :]
    solved[half] = values[half] + at(factor_ref, half) * solved[half - 1]
    for step in range(1, half):
        i = half - 1 - step
        solved[i] = values[i] + at(factor_ref, i) * solved[i + 1]
        i = half + step
        solved[i] = values[i] + at(factor_ref, i) * solved[i - 1]
    for i in range(RADII):
        row = _row_of(i)
        place, zh = row >> 1, row & 1
        out_ref[place, zh : zh + 1, :] = solved[i]
        if i == 0:
            slope = solved[1] * 0.5
        elif i == RADII - 1:
            slope = solved[RADII - 2] * -0.5
        else:
            slope = (solved[i + 1] - solved[i - 1]) * 0.5
        out_ref[place, zh + 2 : zh + 3, :] = slope


def inverse_kernel(x_ref, twist_ref, table_ref, cells_ref, weight_ref, out_ref):
    group = _own_group()
    fields = [[], [], []]
    for n2 in range(8):
        pair = []
        for field in range(2):
            spots = [(n2 * 4 + k, field * 2 + zh) for zh in range(2) for k in range(4)]
            pair.append(jnp.concatenate([x_ref[at, row : row + 1, :] for at, row in spots], axis=0))
        mode = lax.broadcasted_iota(jnp.int32, (8, SECTOR), 1) * 8 + n2
        signed = jnp.where(2 * mode < AZIM, mode, mode - AZIM)
        signed = jnp.where(2 * mode == AZIM, 0, signed).astype(F32)
        fields[0].append(pair[0])
        fields[1].append(pair[1])
        fields[2].append(pair[0] * signed)
    cosine = (table_ref[0:256, :], table_ref[512:768, :])
    sine = (table_ref[256:512, :], table_ref[768:1024, :])
    waves = []
    for field in range(3):
        left = _split(jnp.concatenate(fields[field], axis=0))
        waves.append((_dot3(left, cosine), _dot3(left, sine)))
    for a in range(8):
        tiles = []
        for field in range(3):
            total = None
            for n2 in range(8):
                even = waves[field][0][8 * n2 : 8 * n2 + 8, :]
                odd = waves[field][1][8 * n2 : 8 * n2 + 8, :]
                plus = twist_ref[8 * n2 + a : 8 * n2 + a + 1, :]
                minus = twist_ref[64 + 8 * n2 + a : 65 + 8 * n2 + a, :]
                if field < 2:
                    term = even * plus + odd * minus
                else:
                    term = even * minus - odd * plus
                total = term if total is None else total + term
            for zh in range(2):
                for half in range(2):
                    row = zh * 4 + half * 2
                    out_ref[_group(a, zh), field * 2 + half] = total[row : row + 2, :]
            tiles.append(total)
        accel = [[], [], []]
        for quarter in range(4):
            at = 128 * (quarter % 2)
            cell = [cells_ref[_group(a, zh), 2, quarter // 2 : quarter // 2 + 1, at : at + 128] for zh in range(2)]
            cell = jnp.concatenate([jnp.broadcast_to(part, (4, 128)) for part in cell], axis=0).astype(jnp.int32)
            layer = lax.shift_right_logical(cell, 8)
            lane = cell & 127
            upper = (cell & 128) == 128
            found = [
                jnp.where(upper, _lanes_of(tile[:, 128:], lane), _lanes_of(tile[:, :128], lane))
                for tile in tiles
            ]
            sine_at = _lanes_of(weight_ref[group, 0:8, :], layer)
            step_at = _lanes_of(weight_ref[group, 8:16, :], layer)
            for field, term in enumerate((sine_at * found[1], sine_at * found[2], step_at * found[0])):
                term = term + pltpu.roll(term, 2, axis=0)
                accel[field].append(term + pltpu.roll(term, 1, axis=0))
        for field in range(3):
            for slot, dest, first in ((1, (a + 7) % 8, 0), (0, (a + 1) % 8, 2)):
                pair = jnp.concatenate(accel[field][first : first + 2], axis=1)
                row = slot * 3 + field
                for zh in range(2):
                    spot = 4 * zh + 3
                    out_ref[_group(dest, zh), 6 + row // 2, row % 2 : row % 2 + 1, :] = pair[spot : spot + 1, :]


def pick_kernel(positions_ref, velocities_ref, mass_ref, active_ref, lists_ref, counts_ref, wrap_ref, near_ref):
    wanted = jnp.concatenate([lists_ref[0:1, :], lists_ref[1:2, :]], axis=1)
    total = jnp.zeros((32, 2 * CAP), F32)
    for start in range(0, STARS, CHUNK):
        moving = jnp.concatenate(
            [positions_ref[:, start : start + CHUNK], velocities_ref[:, start : start + CHUNK]], axis=0
        )
        high = moving.astype(BF16).astype(F32)
        rest = moving - high
        middle = rest.astype(BF16).astype(F32)
        low = rest - middle
        plain = jnp.concatenate(
            [
                mass_ref[start : start + CHUNK].astype(F32).reshape(1, CHUNK),
                active_ref[:, start : start + CHUNK].astype(F32),
                jnp.zeros((6, CHUNK), F32),
            ],
            axis=0,
        )
        pad = jnp.zeros((2, CHUNK), F32)
        left = jnp.concatenate([high, pad, middle, pad, low, pad, plain], axis=0).astype(BF16)
        hot = jnp.concatenate([_star_hot(wanted, start), _star_hot(wanted, start + 256)], axis=0)
        total += _dot(left, hot)
    moving = (total[0:6] + total[8:14]) + total[16:22]
    slots = lax.broadcasted_iota(jnp.int32, (1, CAP), 1)
    keep = [jnp.where(slots < counts_ref[:, i : i + 1], 1.0, 0.0) for i in range(2)]
    rows = jnp.concatenate(
        [moving, total[24:25] * jnp.concatenate(keep, axis=1), total[25:26]], axis=0
    )
    down = rows[:, :CAP]
    up = rows[:, CAP:]
    odd = lax.axis_index("a0") == 1
    wrap_ref[...] = jnp.where(odd, up, down)
    near_ref[...] = jnp.where(odd, down, up)


def _sample(fields, layer, angle):
    lanes = layer.shape[1]
    hot = _one_hot(angle, SECTOR)
    both = _dot(fields, hot)
    here = lax.broadcasted_iota(jnp.int32, (HEIGHTS, lanes), 0) == layer
    found = []
    for field in range(3):
        block = both[64 * field : 64 * field + 64] + both[192 + 64 * field : 256 + 64 * field]
        found.append(jnp.sum(jnp.where(here, block, 0.0), axis=0, keepdims=True))
    return found


def _advance(position, velocity, accel, live):
    radius = position[0]
    speed = [
        velocity[0] + live * accel[0],
        velocity[1] + live * (accel[1] / radius),
        velocity[2] + live * accel[2],
    ]
    place = [
        position[0] + live * speed[0],
        position[1] + live * (speed[1] / radius),
        position[2] + live * speed[2],
    ]
    return place + speed


def final_kernel(
    modes_ref, table_ref, close_ref, far_ref, positions_ref, velocities_ref, cells_ref, active_ref,
    grid_ref, state_ref, arrive_ref,
):
    pieces = [modes_ref[group, part] for group in range(16) for part in range(6)]
    modes = jnp.concatenate(pieces, axis=0)
    result = _dot3((table_ref[0:256, :], table_ref[256:512, :]), _split(modes))
    for h in range(HEIGHTS):
        grid_ref[h] = result[h : h + 1, :]
    field_high, field_low = _split(result[64:256])
    fields = jnp.concatenate([field_high, field_low], axis=0)

    sums = []
    for part in range(6, 9):
        total = modes_ref[0, part]
        for group in range(1, 16):
            total = total + modes_ref[group, part]
        sums += [total[0:1], total[1:2]]
    odd = lax.axis_index("a0") == 1
    far = far_ref[...]
    close = close_ref[...]
    for slot in range(2):
        picked = jnp.where(odd, far, close) if slot else jnp.where(odd, close, far)
        state = _advance(
            [picked[i : i + 1] for i in range(3)],
            [picked[i : i + 1] for i in range(3, 6)],
            sums[slot * 3 : slot * 3 + 3],
            picked[7:8],
        )
        keep = picked[6:7] > 0.0
        for row, value in enumerate(state + [picked[6:7]]):
            arrive_ref[row, slot : slot + 1, :] = jnp.where(keep, value, 0.0)

    for start in range(0, STARS, CHUNK):
        lanes = slice(start, start + CHUNK)
        cell = cells_ref[:, lanes]
        accel = _sample(fields, lax.shift_right_logical(cell, 8), cell & 255)
        state = _advance(
            [positions_ref[i : i + 1, lanes] for i in range(3)],
            [velocities_ref[i : i + 1, lanes] for i in range(3)],
            accel,
            active_ref[:, lanes].astype(F32),
        )
        for row in range(6):
            state_ref[row : row + 1, lanes] = state[row]


def _call(kernel, out_shape, name, flops, in_smem=(), in_hbm=(), count=0, scratch=(), limit=48 << 20):
    vmem = pl.BlockSpec(memory_space=pltpu.VMEM)
    smem = pl.BlockSpec(memory_space=pltpu.SMEM)
    hbm = pl.BlockSpec(memory_space=pltpu.HBM)
    outs = jax.tree.map(lambda _: vmem, out_shape)
    return pl.pallas_call(
        kernel,
        out_shape=out_shape,
        in_specs=[smem if i in in_smem else hbm if i in in_hbm else vmem for i in range(count)],
        out_specs=outs,
        scratch_shapes=list(scratch),
        name=name,
        cost_estimate=pl.CostEstimate(flops=flops, bytes_accessed=1 << 20, transcendentals=0),
        compiler_params=pltpu.CompilerParams(vmem_limit_bytes=limit),
    )


def per_device(positions, velocities, masses, cells, active, send_lists, send_counts):
    shape = functools.partial(jax.ShapeDtypeStruct, dtype=F32)
    z_axes, plane_axes = ORDER, PLANE
    exchange = functools.partial(lax.all_to_all, split_axis=0, concat_axis=0, tiled=True)
    table = _split_np(_trig())
    twist = _twist()
    cell = cells.reshape(1, STARS)
    live = active.reshape(1, STARS)

    layered = _call(
        deposit_kernel,
        shape((16, 3, 2, SECTOR)),
        "deposit",
        10**9,
        in_hbm=(0, 1, 2, 3),
        limit=None,
        count=4,
        scratch=[
            pltpu.VMEM((1, STARS), jnp.int32),
            pltpu.VMEM((STARS,), BF16),
            pltpu.VMEM((2, CAP), jnp.int32),
            pltpu.VMEM((STARS // 128, 128), jnp.int32),
            pltpu.SemaphoreType.DMA((4,)),
        ],
    )(cell, masses, send_lists, cells.reshape(STARS // 128, 128))
    layered, eigen, late_lists = lax.optimization_barrier((layered, jnp.asarray(_eigen()), send_lists))
    sectors = exchange(layered, z_axes)
    factors = _call(
        factor_kernel,
        (shape((64, SECTOR)), shape((64, SECTOR)), shape((64, SECTOR)), shape((8, SECTOR))),
        "factor",
        10**9,
        in_smem=(0,),
        count=1,
    )(eigen)
    wrap, near = _call(pick_kernel, (shape((8, CAP)), shape((8, CAP))), "pick", 10**9, count=6)(
        positions, velocities, masses, live, late_lists, send_counts.reshape(1, 2)
    )
    sectors, factors, wrap, near = lax.optimization_barrier((sectors, factors, wrap, near))
    spectrum = _call(forward_kernel, shape((32, 2, SECTOR)), "forward", 10**9, count=3)(
        sectors, twist, table
    )
    columns = exchange(spectrum, plane_axes)
    solved = _call(
        solve_kernel,
        shape((32, 4, SECTOR)),
        "solve",
        10**9,
        count=5,
        scratch=[pltpu.VMEM((64, SECTOR), F32)],
    )(columns, *factors)
    waves = exchange(solved, plane_axes)
    angles = _call(inverse_kernel, shape((16, 9, 2, SECTOR)), "inverse", 10**9, count=5)(
        waves, twist, table, sectors, _weight_table()
    )
    angles, wrap, near = lax.optimization_barrier((angles, wrap, near))
    modes = exchange(angles, z_axes)
    close = lax.ppermute(near, AZ, [(i, i ^ 1) for i in range(8)])
    far = lax.ppermute(wrap, AZ, [(i, (i + 1) % 8 if i % 2 else (i + 7) % 8) for i in range(8)])
    potential, state, arrivals = _call(
        final_kernel,
        (shape((64, 1, SECTOR)), shape((6, STARS)), shape((7, 2, CAP))),
        "final",
        10**9,
        count=8,
    )(modes, _split_np(_field_table()), close, far, positions, velocities, cell, live)
    return potential, state, arrivals.transpose(1, 0, 2)


def solution(mesh):
    fine = Mesh(mesh.devices.reshape(2, 2, 2, 2, 2, 2, 2, 2, 2), ("a2", "a1", "a0", "x1", "x0", "zh", "y1", "y0", "c"))
    rz = ("x1", "x0", "zh", "y1", "y0", "c")
    every = AZ + rz
    return jax.shard_map(
        per_device,
        mesh=fine,
        in_specs=(
            P(None, every),
            P(None, every),
            P(every),
            P(every),
            P(every),
            P(None, every),
            P(None, every),
        ),
        out_specs=(P(None, rz, AZ), P(None, every), P(None, None, every)),
        check_vma=False,
    )
```
